256 devices in a mesh: tm: 8 (over z), lat: 32 (over y, x, core).
Axes of the slice: x: 4, y: 4, z: 8, core: 2. Of those that a mesh axis runs over, the one named last changes fastest.
Arguments:
- wind_east: bfloat16 [960, 256, 1440], P('tm', 'lat'), may hold values from -40 to 40
- wind_north: bfloat16 [960, 256, 1440], P('tm', 'lat'), may hold values from -40 to 40
- snap_counts: int32 [8], P('tm'), may hold values from 1 to 120, 320 in all
- snap_ids: int32 [960], P('tm'), may hold values from 0 to 8759
Outputs:
- basis: bfloat16 [32, 256, 1440], P(None, 'lat')
- coeffs: float32 [32, 960], P(None, 'tm')
The draws below stay inside these ranges and needn't reach their ends.
Inputs may be any that keep to these rules, and one draw needn't show every extreme that they name: `snap_counts`: entry b counts the used slots of the b-th block of 120 slots, which are that block's first ones; the entries sum to 320 and one of them equals 120.
All inputs are finite; a program needn't handle non-finite values.
Results may differ from the reference program's by a relative error of at most 0.0072.
Values may be sent and summed in bfloat16 or wider, within the bound.
A program may use at most 64 MiB of HBM per device.

```python
import math
import jax
import jax.numpy as jnp
import numpy as np
from jax import lax

NLON = 1440
RANK = 32
SNAP_MAX = 120
SNAP_MEAN = 40
NLAT = 256
SNAPS = 960
CELLS = 368640
N_TM = 8


def wind_field(key, salt):
    keys = jax.random.split(jax.random.fold_in(key, salt), 5)
    modes = jax.random.normal(keys[0], (4, NLAT, NLON), jnp.float32)
    amplitude = jax.random.normal(keys[1], (SNAPS, 4), jnp.float32)
    noise = jax.random.normal(keys[2], (SNAPS, NLAT, NLON), jnp.float32)
    common = 0.5
    shared = jnp.einsum('sk,kab->sab', amplitude, modes)
    base = (common * shared + noise) / jnp.sqrt(1.0 + 4.0 * common * common)
    row_place = jnp.arange(NLAT, dtype=jnp.float32) / NLAT
    row_scale = 10.0 ** (0.5 * row_place + 0.5 * jax.random.uniform(keys[3], (NLAT,), jnp.float32)) / jnp.sqrt(10.0)
    snap_scale = 10.0 ** (jax.random.uniform(keys[4], (SNAPS,), jnp.float32) - 0.5)
    values = base * row_scale[None, :, None] * snap_scale[:, None, None]
    return jnp.clip(values, -40.0, 40.0)


def draw_wind_east(key, part):
    return wind_field(key, 11).astype(jnp.bfloat16)


def draw_wind_north(key, part):
    return wind_field(key, 23).astype(jnp.bfloat16)


def with_ends(drawn, own_key, low, top_value):
    shape = drawn.shape
    spot = [jax.random.randint(jax.random.fold_in(own_key, axis), (), 0, shape[axis]) for axis in range(len(shape))]
    drawn = drawn.at[tuple(spot)].set(low)
    longest = shape.index(max(shape))
    spot[longest] = (spot[longest] + 1) % shape[longest]
    return drawn.at[tuple(spot)].set(top_value)


def length_profile(number_of, total, reach, slope):
    portions = [(1 << 20) // math.isqrt(grade ** slope) + 1 for grade in range(2, number_of + 1)]
    spare, holding = total - reach - (number_of - 1), [1] * (number_of - 1)
    while spare > 0:
        candidates = [i for i in range(number_of - 1) if holding[i] < reach]
        whole, budget = sum([portions[i] for i in candidates]), spare
        for i in candidates:
            more = min(reach - holding[i], max(1, budget * portions[i] // whole), spare)
            holding[i] = holding[i] + more
            spare = spare - more
    return np.array([reach] + holding)


def uneven(key, number_of, total, reach, slope):
    if number_of == 2:
        one = jax.random.randint(key, (), max(1, total - reach), min(reach, total - 1) + 1)
        return jnp.stack([one, total - one])
    lengths = jnp.asarray(length_profile(number_of, total, reach, slope), jnp.int32)
    couples = (number_of - 1) // 2
    source_of, sink = lengths[1:1 + 2 * couples:2], lengths[2:2 + 2 * couples:2]
    margin = jnp.minimum(source_of - 1, reach - sink)
    shifted = jax.random.randint(jax.random.fold_in(key, 1), (couples,), 0, 1 << 20) % (margin + 1)
    lengths = lengths.at[1:1 + 2 * couples:2].set(source_of - shifted).at[2:2 + 2 * couples:2].set(sink + shifted)
    return lengths[jax.random.permutation(jax.random.fold_in(key, 2), number_of)]


def setup_inputs(seed: int = 0) -> dict:
    key_list = jax.random.split(jax.random.key(seed), 5)
    return {
        "wind_east": draw_wind_east(jax.random.fold_in(key_list[4], 71), 0),
        "wind_north": draw_wind_north(jax.random.fold_in(key_list[4], 71), 0),
        "snap_counts": uneven(key_list[2], N_TM, SNAP_MEAN * N_TM, SNAP_MAX, 2).astype(jnp.int32),
        "snap_ids": with_ends(jax.random.randint(key_list[3], (SNAPS,), 0, 8760), jax.random.fold_in(key_list[3], 1), 0, 8759).astype(jnp.int32),
    }


def latitude_cosine(first_row, row_count, total_rows):
    row_index = first_row + jnp.arange(row_count, dtype=jnp.int32)
    return jnp.cos((total_rows // 2 - row_index).astype(jnp.float32) * (jnp.pi / 720.0))

def sign_table(snap_ids, rank_count):
    column = jnp.arange(rank_count, dtype=jnp.int32)
    mixed = snap_ids[:, None] * 1103515245 + column[None, :] * 40503 + 12345
    mixed = jnp.bitwise_xor(mixed, jnp.right_shift(mixed, 13))
    mixed = mixed * 1664525 + 1013904223
    mixed = jnp.bitwise_xor(mixed, jnp.right_shift(mixed, 16))
    flipped = jnp.bitwise_and(jnp.right_shift(mixed, 7), 1)
    return (1 - 2 * flipped).astype(jnp.bfloat16)

def metric_vorticity(padded_east, wind_north, padded_cosine, valid):
    scaled = padded_east.astype(jnp.float32) * padded_cosine[None, :, None]
    north_side = scaled[:, :-2]
    south_side = scaled[:, 2:]
    meridional = wind_north.astype(jnp.float32)
    zonal_diff = jnp.roll(meridional, -1, axis=2) - jnp.roll(meridional, 1, axis=2)
    weight = 0.5 / jnp.sqrt(padded_cosine[1:-1])
    field = (zonal_diff - north_side + south_side) * weight[None, :, None] * valid[:, None, None]
    return field.astype(jnp.bfloat16)

def reference(wind_east, wind_north, snap_counts, snap_ids):
    slot_index = jnp.arange(SNAPS, dtype=jnp.int32)
    valid_all = (slot_index % SNAP_MAX < snap_counts[slot_index // SNAP_MAX]).astype(jnp.float32)
    padded_cosine = latitude_cosine(-1, NLAT + 2, NLAT)
    signs_all = sign_table(snap_ids, RANK)
    east_blocks = wind_east.reshape(N_TM, SNAP_MAX, NLAT, NLON)
    north_blocks = wind_north.reshape(N_TM, SNAP_MAX, NLAT, NLON)
    valid_blocks = valid_all.reshape(N_TM, SNAP_MAX)
    sign_blocks = signs_all.reshape(N_TM, SNAP_MAX, RANK)

    def block_field(block):
        padded = jnp.pad(east_blocks[block], ((0, 0), (1, 1), (0, 0)))
        field = metric_vorticity(padded, north_blocks[block], padded_cosine, valid_blocks[block])
        return field.reshape(SNAP_MAX, NLAT * NLON)

    def accumulate(total, block):
        field = block_field(block)
        return (total + jnp.dot(sign_blocks[block].T.astype(jnp.float32), field.astype(jnp.float32), preferred_element_type=jnp.float32), None)
    block_list = jnp.arange(N_TM, dtype=jnp.int32)
    sketch, _ = lax.scan(accumulate, jnp.zeros((RANK, NLAT * NLON), jnp.float32), block_list)
    gram_sum = lax.dot_general(sketch.astype(jnp.float32), sketch.astype(jnp.float32), (((1,), (1,)), ((), ())), precision=lax.Precision.HIGHEST, preferred_element_type=jnp.float32) / CELLS
    factor = jnp.linalg.cholesky(gram_sum)
    inverse = lax.linalg.triangular_solve(factor, jnp.eye(RANK, dtype=jnp.float32), left_side=True, lower=True)
    basis_flat = jnp.dot(inverse.astype(jnp.float32), sketch.astype(jnp.float32), precision=lax.Precision.HIGHEST, preferred_element_type=jnp.float32).astype(jnp.bfloat16)

    def project(block):
        field = block_field(block)
        return lax.dot_general(basis_flat.astype(jnp.float32), field.astype(jnp.float32), (((1,), (1,)), ((), ())), preferred_element_type=jnp.float32) / CELLS
    projected = lax.map(project, block_list)
    coeffs = jnp.transpose(projected, (1, 0, 2)).reshape(RANK, SNAPS)
    return (basis_flat.reshape(RANK, NLAT, NLON), coeffs)
```

```python
import functools

import jax
import jax.numpy as jnp
import numpy as np
from jax import lax
from jax.experimental import pallas as pl
from jax.experimental.pallas import tpu as pltpu
from jax.sharding import PartitionSpec as P

RANK = 32
LANE = 128
F32 = jnp.float32
BF16 = jnp.bfloat16
MESH = pl.DeviceIdType.MESH
HIGHEST = lax.Precision.HIGHEST
NSUB = 4
NLOAD = 5


def dot(a, b, precision=None):
    return lax.dot_general(
        a, b, (((1,), (0,)), ((), ())), precision=precision, preferred_element_type=F32
    )


def dot_t(a, b, precision=None):
    return lax.dot_general(
        a, b, (((1,), (1,)), ((), ())), precision=precision, preferred_element_type=F32
    )


def iota(shape, dim):
    return lax.broadcasted_iota(jnp.int32, shape, dim)


def split(x):
    high = x.astype(BF16)
    return high, (x - high.astype(F32)).astype(BF16)


def cosine(x):
    y = x * x
    p = jnp.full_like(y, -1.0 / 3628800.0)
    for coefficient in (1.0 / 40320.0, -1.0 / 720.0, 1.0 / 24.0, -0.5, 1.0):
        p = p * y + coefficient
    return p


def inverse_factor(gram):
    row, lane = iota((RANK, LANE), 0), iota((RANK, LANE), 1)
    a = jnp.where(lane == row + RANK, 1.0, gram)
    for k in range(RANK - 1):
        pivot_row = a[k : k + 1, :]
        column = a[:, k : k + 1]
        factor = column / a[k : k + 1, k : k + 1]
        a = a - jnp.where(row > k, factor * pivot_row, 0.0)
    diagonal = jnp.sum(jnp.where(row == lane, a, 0.0), axis=1, keepdims=True)
    scaled = a * lax.rsqrt(diagonal)
    return pltpu.roll(scaled, LANE - RANK, 1)[:, :RANK]


def kernel(
    shape,
    east_hbm,
    north_hbm,
    count_ref,
    ids_ref,
    basis_ref,
    coeffs_ref,
    east_raw,
    north_raw,
    east_f,
    north_f,
    edge_send,
    edge_recv,
    field,
    sketch,
    minus_send,
    minus_recv,
    plus_send,
    plus_recv,
    whole,
    grams,
    mine,
    pair_recv,
    x_slots,
    y_slots,
    load_sem,
    edge_ssem,
    edge_rsem,
    minus_ssem,
    minus_rsem,
    plus_ssem,
    plus_rsem,
    gm_ssem,
    gm_rsem,
    gp_ssem,
    gp_rsem,
    pair_sem,
    x_ssem,
    x_rsem,
    y_ssem,
    y_rsem,
):
    slots, rows, lons, n_tm, n_lat, n_x = shape
    n_y = n_lat // (2 * n_x)
    n_col = pl.cdiv(lons, LANE)
    tail = lons - (n_col - 1) * LANE
    padded = field.shape[1]
    width = n_col * LANE
    piece = width // NSUB
    total_rows = rows * n_lat
    cells = total_rows * lons

    m = lax.axis_index("tm")
    b = lax.axis_index("lat")
    core = lax.rem(b, 2)
    x = lax.rem(b // 2, n_x)
    y = b // (2 * n_x)
    z_plus, z_minus = {"tm": lax.rem(m + 1, n_tm)}, {"tm": lax.rem(m + n_tm - 1, n_tm)}
    south, north = {"lat": lax.rem(b + 1, n_lat)}, {"lat": lax.rem(b + n_lat - 1, n_lat)}
    partner = {"lat": b + 1 - 2 * core}

    def x_peer(d):
        return {"lat": (y * n_x + lax.rem(x + d, n_x)) * 2 + core}

    def y_peer(d):
        return {"lat": (lax.rem(y + d, n_y) * n_x + x) * 2 + core}

    peers = [z_plus, z_minus, south, north, partner]
    peers += [x_peer(d) for d in range(1, n_x)] + [y_peer(d) for d in range(1, n_y)]
    barrier = pltpu.get_barrier_semaphore()
    for peer in peers:
        pl.semaphore_signal(barrier, inc=1, device_id=peer, device_id_type=MESH)

    def remote(src, dst, ssem, rsem, peer):
        return pltpu.make_async_remote_copy(
            src_ref=src, dst_ref=dst, send_sem=ssem, recv_sem=rsem, device_id=peer, device_id_type=MESH
        )

    chunk = slots // NLOAD
    loads = []
    for which, (src, dst) in enumerate(((east_hbm, east_raw), (north_hbm, north_raw))):
        for i in range(NLOAD):
            part = pl.ds(i * chunk, chunk)
            copy = pltpu.make_async_copy(src.at[part], dst.at[part], load_sem.at[which, i])
            copy.start()
            loads.append(copy)

    ids = jnp.broadcast_to(ids_ref[...], (RANK, padded))
    column = iota((RANK, padded), 0)
    mixed = ids * 1103515245 + column * 40503 + 12345
    mixed = jnp.bitwise_xor(mixed, jnp.right_shift(mixed, 13))
    mixed = mixed * 1664525 + 1013904223
    mixed = jnp.bitwise_xor(mixed, jnp.right_shift(mixed, 16))
    flipped = jnp.bitwise_and(jnp.right_shift(mixed, 7), 1)
    slot_used = iota((RANK, padded), 1) < count_ref[0]
    signs = jnp.where(slot_used, (1 - 2 * flipped).astype(F32), 0.0).astype(BF16)

    band_row = iota((16, LANE), 0) + (b * rows - 1)
    cosines = cosine((total_rows // 2 - band_row).astype(F32) * (jnp.pi / 720.0))
    weights = 0.5 / jnp.sqrt(cosines)
    inside = jnp.logical_and(band_row >= 0, band_row < total_rows)
    cosines = jnp.where(inside, cosines, 0.0)

    zero_rows = padded * rows - slots * rows
    for store in (east_f, north_f):
        store[:, slots * rows :, :] = jnp.zeros((n_col, zero_rows, LANE), F32)
        store[n_col - 1] = jnp.zeros((padded * rows, LANE), F32)

    def widen(raw, store, copies):
        for i in range(NLOAD):
            copies[i].wait()
            for c in range(n_col):
                w = LANE if c < n_col - 1 else tail
                value = raw[i * chunk : (i + 1) * chunk, :, c * LANE : c * LANE + w]
                store[c, i * chunk * rows : (i + 1) * chunk * rows, 0:w] = value.astype(F32).reshape(
                    chunk * rows, w
                )

    widen(east_raw, east_f, loads[:NLOAD])
    for side, j in ((0, 0), (1, rows - 1)):
        for c in range(n_col):
            edge_send[side, :, c * LANE : (c + 1) * LANE] = east_f[c, pl.ds(j, padded, stride=rows), :].astype(
                BF16
            )
    pl.semaphore_wait(barrier, len(peers))
    edges = [
        remote(edge_send.at[0], edge_recv.at[1], edge_ssem.at[0], edge_rsem.at[1], north),
        remote(edge_send.at[1], edge_recv.at[0], edge_ssem.at[1], edge_rsem.at[0], south),
    ]
    for copy in edges:
        copy.start()
    widen(north_raw, north_f, loads[NLOAD:])

    lane16 = iota((16, LANE), 1)

    def field_row(j, east_above, east_below, c_above, c_below, weight):
        def group(g, carry):
            part = pl.ds(g * (16 * rows) + j, 16, stride=rows)
            w = [north_f[c, part, :] for c in range(n_col)]
            left = [pltpu.roll(t, LANE - 1, 1) for t in w]
            right = [pltpu.roll(t, 1, 1) for t in w]
            first_to_end = pltpu.roll(w[0], tail - 1, 1)
            end_to_first = pltpu.roll(w[-1], LANE - tail + 1, 1)
            for c in range(n_col):
                if c < n_col - 1:
                    nxt = jnp.where(lane16 < LANE - 1, left[c], left[c + 1])
                else:
                    nxt = jnp.where(lane16 < tail - 1, left[c], first_to_end)
                prv = jnp.where(lane16 > 0, right[c], right[c - 1] if c > 0 else end_to_first)
                value = (
                    (nxt - prv) - east_above(g, c) * c_above + east_below(g, c) * c_below
                ) * weight
                if c == n_col - 1:
                    value = jnp.where(lane16 < tail, value, 0.0)
                field[j, pl.ds(g * 16, 16), c * LANE : (c + 1) * LANE] = value.astype(BF16)
            return carry

        lax.fori_loop(0, padded // 16, group, 0)
        sketch[j] = dot(signs, field[j])

    def local_east(j):
        return lambda g, c: east_f[c, pl.ds(g * (16 * rows) + j, 16, stride=rows), :]

    def halo_east(side):
        return lambda g, c: edge_recv[side, pl.ds(g * 16, 16), c * LANE : (c + 1) * LANE].astype(F32)

    def table(t, i):
        return jnp.broadcast_to(t[i : i + 1, :], (16, LANE))

    for j in range(1, rows - 1):
        field_row(j, local_east(j - 1), local_east(j + 1), table(cosines, j), table(cosines, j + 2), table(weights, j + 1))
    edges[1].wait_recv()
    edges[0].wait_recv()
    j = 0
    field_row(j, halo_east(0), local_east(j + 1), table(cosines, j), table(cosines, j + 2), table(weights, j + 1))
    j = rows - 1
    field_row(j, local_east(j - 1), halo_east(1), table(cosines, j), table(cosines, j + 2), table(weights, j + 1))

    hops_minus, hops_plus = n_tm // 2, n_tm // 2 - 1

    def cols(h):
        return pl.ds(h * piece, piece)

    def chain(send, recv, ssem, rsem, peer, k, h):
        return remote(
            send.at[k, :, cols(h)], recv.at[k, :, cols(h)], ssem.at[k, h], rsem.at[k, h], peer
        )

    minus = functools.partial(chain, minus_send, minus_recv, minus_ssem, minus_rsem, z_minus)
    plus = functools.partial(chain, plus_send, plus_recv, plus_ssem, plus_rsem, z_plus)
    for k in range(hops_minus):
        for name, copy, send, recv, hops, j in (
            ("minus", minus, minus_send, minus_recv, hops_minus, lax.rem(m + hops_minus + k, n_tm)),
            ("plus", plus, plus_send, plus_recv, hops_plus, lax.rem(m + n_tm + hops_plus - k, n_tm)),
        ):
            if k >= hops:
                continue
            for h in range(NSUB):
                value = sketch[j, :, cols(h)]
                if k > 0:
                    copy(k - 1, h).wait_recv()
                    value = value + recv[k - 1, :, cols(h)].astype(F32)
                send[k, :, cols(h)] = value.astype(BF16)
                copy(k, h).start()

    def gather(ssem, rsem, peer, k, h, j):
        return remote(
            whole.at[j, :, cols(h)], whole.at[j, :, cols(h)], ssem.at[k, h], rsem.at[k, h], peer
        )

    to_minus = functools.partial(gather, gm_ssem, gm_rsem, z_minus)
    to_plus = functools.partial(gather, gp_ssem, gp_rsem, z_plus)
    for h in range(NSUB):
        plus(hops_plus - 1, h).wait_recv()
        minus(hops_minus - 1, h).wait_recv()
        value = sketch[m, :, cols(h)] + plus_recv[hops_plus - 1, :, cols(h)].astype(F32)
        value = value + minus_recv[hops_minus - 1, :, cols(h)].astype(F32)
        whole[m, :, cols(h)] = value.astype(BF16)
        to_minus(0, h, m).start()
        to_plus(0, h, m).start()

    mine[...] = jnp.zeros(mine.shape, F32)

    def consume(j):
        value = whole[j]
        mine[0:RANK, :] += dot_t(value, field[j])
        grams[j] = dot_t(value, value)

    consume(m)
    for k in range(1, hops_minus + 1):
        j_minus = lax.rem(m + k, n_tm)
        j_plus = lax.rem(m + n_tm - k, n_tm)
        for h in range(NSUB):
            to_minus(k - 1, h, j_minus).wait_recv()
            if k < hops_minus:
                to_minus(k, h, j_minus).start()
        if k <= hops_plus:
            for h in range(NSUB):
                to_plus(k - 1, h, j_plus).wait_recv()
                if k < hops_plus:
                    to_plus(k, h, j_plus).start()
        consume(j_minus)
        if k <= hops_plus:
            consume(j_plus)

    gram = grams[0]
    for j in range(1, rows):
        gram = gram + grams[j]
    mine[RANK : 2 * RANK, 0:RANK] = gram

    pair = remote(mine, pair_recv, pair_sem.at[0], pair_sem.at[1], partner)
    pair.start()
    pair.wait_recv()
    value = mine[...] + pair_recv[...]
    for store, ssem, rsem, count, here, peer_of in (
        (x_slots, x_ssem, x_rsem, n_x, x, x_peer),
        (y_slots, y_ssem, y_rsem, n_y, y, y_peer),
    ):
        store[here] = value
        for d in range(1, count):
            remote(store.at[here], store.at[here], ssem.at[d - 1], rsem.at[d - 1], peer_of(d)).start()
        for d in range(1, count):
            origin = lax.rem(here + count - d, count)
            remote(store.at[origin], store.at[origin], ssem.at[d - 1], rsem.at[d - 1], peer_of(d)).wait_recv()
        value = store[0]
        for i in range(1, count):
            value = value + store[i]

    projected = value[0:RANK, :]
    inverse = inverse_factor(value[RANK : 2 * RANK, :] * (1.0 / cells))
    coeffs = dot(inverse, projected, HIGHEST) * (1.0 / cells)
    coeffs = jnp.where(iota((RANK, padded), 1) < count_ref[0], coeffs, 0.0)
    coeffs_ref[...] = coeffs[:, :slots]

    size = RANK * rows
    take_row = (iota((size, RANK), 0) // rows == iota((size, RANK), 1)).astype(F32).astype(BF16)
    take_col = (iota((RANK, size), 0) == lax.rem(iota((RANK, size), 1), RANK)).astype(F32).astype(BF16)
    same = lax.rem(iota((size, size), 0), rows) == iota((size, size), 1) // RANK
    flat = whole[...].reshape(size, width)
    basis = None
    for half in split(inverse):
        spread = dot(take_row, half).astype(BF16)
        spread = dot(spread, take_col)
        spread = jnp.where(same, spread, 0.0).astype(BF16)
        term = dot(spread, flat)
        basis = term if basis is None else basis + term
    basis_ref[...] = basis.reshape(RANK, rows, width)[:, :, :lons].astype(BF16)

    for copy in edges:
        copy.wait_send()
    for h in range(NSUB):
        for k in range(hops_minus):
            minus(k, h).wait_send()
            to_minus(k, h, m).wait_send()
        for k in range(hops_plus):
            plus(k, h).wait_send()
            to_plus(k, h, m).wait_send()
    pair.wait_send()
    for store, ssem, rsem, count, here, peer_of in (
        (x_slots, x_ssem, x_rsem, n_x, x, x_peer),
        (y_slots, y_ssem, y_rsem, n_y, y, y_peer),
    ):
        for d in range(1, count):
            remote(store.at[here], store.at[here], ssem.at[d - 1], rsem.at[d - 1], peer_of(d)).wait_send()


def local(n_tm, n_lat, n_x, wind_east, wind_north, snap_counts, snap_ids):
    slots, rows, lons = wind_east.shape
    padded = -(-slots // LANE) * LANE
    n_col = -(-lons // LANE)
    width = n_col * LANE
    n_y = n_lat // (2 * n_x)
    ids = jnp.pad(snap_ids, (0, padded - slots)).reshape(1, padded)
    shape = (slots, rows, lons, n_tm, n_lat, n_x)
    hm, hp = n_tm // 2, n_tm // 2 - 1
    dma = pltpu.SemaphoreType.DMA
    return pl.pallas_call(
        functools.partial(kernel, shape),
        out_shape=(
            jax.ShapeDtypeStruct((RANK, rows, lons), BF16),
            jax.ShapeDtypeStruct((RANK, slots), F32),
        ),
        in_specs=[
            pl.BlockSpec(memory_space=pl.ANY),
            pl.BlockSpec(memory_space=pl.ANY),
            pl.BlockSpec(memory_space=pltpu.SMEM),
            pl.BlockSpec(memory_space=pltpu.VMEM),
        ],
        out_specs=(pl.BlockSpec(memory_space=pltpu.VMEM), pl.BlockSpec(memory_space=pltpu.VMEM)),
        scratch_shapes=[
            pltpu.VMEM((slots, rows, lons), BF16),
            pltpu.VMEM((slots, rows, lons), BF16),
            pltpu.VMEM((n_col, padded * rows, LANE), F32),
            pltpu.VMEM((n_col, padded * rows, LANE), F32),
            pltpu.VMEM((2, padded, width), BF16),
            pltpu.VMEM((2, padded, width), BF16),
            pltpu.VMEM((rows, padded, width), BF16),
            pltpu.VMEM((rows, RANK, width), F32),
            pltpu.VMEM((hm, RANK, width), BF16),
            pltpu.VMEM((hm, RANK, width), BF16),
            pltpu.VMEM((hp, RANK, width), BF16),
            pltpu.VMEM((hp, RANK, width), BF16),
            pltpu.VMEM((rows, RANK, width), BF16),
            pltpu.VMEM((rows, RANK, RANK), F32),
            pltpu.VMEM((2 * RANK, LANE), F32),
            pltpu.VMEM((2 * RANK, LANE), F32),
            pltpu.VMEM((n_x, 2 * RANK, LANE), F32),
            pltpu.VMEM((n_y, 2 * RANK, LANE), F32),
            dma((2, NLOAD)),
            dma((2,)),
            dma((2,)),
            dma((hm, NSUB)),
            dma((hm, NSUB)),
            dma((hp, NSUB)),
            dma((hp, NSUB)),
            dma((hm, NSUB)),
            dma((hm, NSUB)),
            dma((hp, NSUB)),
            dma((hp, NSUB)),
            dma((2,)),
            dma((n_x - 1,)),
            dma((n_x - 1,)),
            dma((n_y - 1,)),
            dma((n_y - 1,)),
        ],
        compiler_params=pltpu.CompilerParams(
            collective_id=0, has_side_effects=True, vmem_limit_bytes=60 * 1024 * 1024
        ),
        name="eof",
    )(wind_east, wind_north, snap_counts, ids)


def solution(mesh):
    in_specs = (P("tm", "lat", None), P("tm", "lat", None), P("tm"), P("tm"))
    out_specs = (P(None, "lat", None), P(None, "tm"))
    body = functools.partial(local, mesh.shape["tm"], mesh.shape["lat"], 4)
    return jax.shard_map(body, mesh=mesh, in_specs=in_specs, out_specs=out_specs, check_vma=False)
```

```python
import functools

import jax
import jax.numpy as jnp
import numpy as np
from jax import lax
from jax.experimental import pallas as pl
from jax.experimental.pallas import tpu as pltpu
from jax.sharding import PartitionSpec as P

RANK = 32
LANE = 128
F32 = jnp.float32
BF16 = jnp.bfloat16
MESH = pl.DeviceIdType.MESH
HIGHEST = lax.Precision.HIGHEST
NSUB = 4
NLOAD = 5


def dot(a, b, precision=None):
    return lax.dot_general(
        a, b, (((1,), (0,)), ((), ())), precision=precision, preferred_element_type=F32
    )


def dot_t(a, b, precision=None):
    return lax.dot_general(
        a, b, (((1,), (1,)), ((), ())), precision=precision, preferred_element_type=F32
    )


def iota(shape, dim):
    return lax.broadcasted_iota(jnp.int32, shape, dim)


def split(x):
    high = x.astype(BF16)
    return high, (x - high.astype(F32)).astype(BF16)


def cosine(x):
    y = x * x
    p = jnp.full_like(y, -1.0 / 3628800.0)
    for coefficient in (1.0 / 40320.0, -1.0 / 720.0, 1.0 / 24.0, -0.5, 1.0):
        p = p * y + coefficient
    return p


def inverse_factor(gram):
    row, lane = iota((RANK, LANE), 0), iota((RANK, LANE), 1)
    a = jnp.where(lane == row + RANK, 1.0, gram)
    for k in range(RANK - 1):
        pivot_row = a[k : k + 1, :]
        column = a[:, k : k + 1]
        factor = column / a[k : k + 1, k : k + 1]
        a = a - jnp.where(row > k, factor * pivot_row, 0.0)
    diagonal = jnp.sum(jnp.where(row == lane, a, 0.0), axis=1, keepdims=True)
    scaled = a * lax.rsqrt(diagonal)
    return pltpu.roll(scaled, LANE - RANK, 1)[:, :RANK]


def kernel(
    shape,
    east_hbm,
    north_hbm,
    count_ref,
    ids_ref,
    basis_ref,
    coeffs_ref,
    east_raw,
    north_raw,
    east_f,
    north_f,
    edge_send,
    edge_recv,
    field,
    sketch,
    tables,
    chain_send,
    chain_recv,
    whole,
    grams,
    mine,
    pair_recv,
    x_slots,
    y_slots,
    load_sem,
    edge_ssem,
    edge_rsem,
    chain_ssem,
    chain_rsem,
    gather_ssem,
    gather_rsem,
    pair_sem,
    x_ssem,
    x_rsem,
    y_ssem,
    y_rsem,
):
    slots, rows, lons, n_tm, n_lat, n_x = shape
    n_y = n_lat // (2 * n_x)
    n_col = pl.cdiv(lons, LANE)
    tail = lons - (n_col - 1) * LANE
    padded = field.shape[1]
    width = n_col * LANE
    piece = width // NSUB
    total_rows = rows * n_lat
    cells = total_rows * lons

    m = lax.axis_index("tm")
    b = lax.axis_index("lat")
    core = lax.rem(b, 2)
    x = lax.rem(b // 2, n_x)
    y = b // (2 * n_x)
    z_plus, z_minus = {"tm": lax.rem(m + 1, n_tm)}, {"tm": lax.rem(m + n_tm - 1, n_tm)}
    south, north = {"lat": lax.rem(b + 1, n_lat)}, {"lat": lax.rem(b + n_lat - 1, n_lat)}
    partner = {"lat": b + 1 - 2 * core}

    def x_peer(d):
        return {"lat": (y * n_x + lax.rem(x + d, n_x)) * 2 + core}

    def y_peer(d):
        return {"lat": (lax.rem(y + d, n_y) * n_x + x) * 2 + core}

    peers = [z_plus, z_minus, south, north, partner]
    peers += [x_peer(d) for d in range(1, n_x)] + [y_peer(d) for d in range(1, n_y)]
    barrier = pltpu.get_barrier_semaphore()
    for peer in peers:
        pl.semaphore_signal(barrier, inc=1, device_id=peer, device_id_type=MESH)

    def remote(src, dst, ssem, rsem, peer):
        return pltpu.make_async_remote_copy(
            src_ref=src, dst_ref=dst, send_sem=ssem, recv_sem=rsem, device_id=peer, device_id_type=MESH
        )

    chunk = slots // NLOAD
    loads = []
    for which, (src, dst) in enumerate(((east_hbm, east_raw), (north_hbm, north_raw))):
        for i in range(NLOAD):
            part = pl.ds(i * chunk, chunk)
            copy = pltpu.make_async_copy(src.at[part], dst.at[part], load_sem.at[which, i])
            copy.start()
            loads.append(copy)

    ids = jnp.broadcast_to(ids_ref[...], (RANK, padded))
    column = iota((RANK, padded), 0)
    mixed = ids * 1103515245 + column * 40503 + 12345
    mixed = jnp.bitwise_xor(mixed, jnp.right_shift(mixed, 13))
    mixed = mixed * 1664525 + 1013904223
    mixed = jnp.bitwise_xor(mixed, jnp.right_shift(mixed, 16))
    flipped = jnp.bitwise_and(jnp.right_shift(mixed, 7), 1)
    slot_used = iota((RANK, padded), 1) < count_ref[0]
    signs = jnp.where(slot_used, (1 - 2 * flipped).astype(F32), 0.0).astype(BF16)

    band_row = iota((16, LANE), 0) + (b * rows - 1)
    cosines = cosine((total_rows // 2 - band_row).astype(F32) * (jnp.pi / 720.0))
    weights = 0.5 / jnp.sqrt(cosines)
    inside = jnp.logical_and(band_row >= 0, band_row < total_rows)
    tables[0] = jnp.where(inside, cosines, 0.0)
    tables[1] = weights

    zero_rows = padded * rows - slots * rows
    for store in (east_f, north_f):
        store[:, slots * rows : padded * rows, :] = jnp.zeros((n_col, zero_rows, LANE), F32)
        store[n_col - 1, 0 : padded * rows, :] = jnp.zeros((padded * rows, LANE), F32)

    def widen(raw, store, copies):
        for i in range(NLOAD):
            copies[i].wait()
            for c in range(n_col):
                w = LANE if c < n_col - 1 else tail
                value = raw[i * chunk : (i + 1) * chunk, :, c * LANE : c * LANE + w]
                store[c, i * chunk * rows : (i + 1) * chunk * rows, 0:w] = value.astype(F32).reshape(
                    chunk * rows, w
                )

    widen(east_raw, east_f, loads[:NLOAD])
    for side, j in ((0, 0), (1, rows - 1)):
        for c in range(n_col):
            edge_send[side, :, c * LANE : (c + 1) * LANE] = east_f[c, pl.ds(j, padded, stride=rows), :].astype(
                BF16
            )
    widen(north_raw, north_f, loads[NLOAD:])

    pl.semaphore_wait(barrier, len(peers))
    edges = [
        remote(edge_send.at[0], edge_recv.at[1], edge_ssem.at[0], edge_rsem.at[1], north),
        remote(edge_send.at[1], edge_recv.at[0], edge_ssem.at[1], edge_rsem.at[0], south),
    ]
    for copy in edges:
        copy.start()

    lane16 = iota((16, LANE), 1)

    def compute_row(j):
        above = jnp.where(j > 0, j - 1, padded * rows)
        below = jnp.where(j < rows - 1, j + 1, padded * rows + 1)

        def table(t, i):
            return jnp.broadcast_to(tables[t, pl.ds(i, 1), :], (16, LANE))

        c_above, c_below, weight = table(0, j), table(0, j + 2), table(1, j + 1)

        def group(g, carry):
            def part(first):
                return pl.ds(g * (16 * rows) + first, 16, stride=rows)

            w = [north_f[c, part(j), :] for c in range(n_col)]
            left = [pltpu.roll(t, LANE - 1, 1) for t in w]
            right = [pltpu.roll(t, 1, 1) for t in w]
            first_to_end = pltpu.roll(w[0], tail - 1, 1)
            end_to_first = pltpu.roll(w[-1], LANE - tail + 1, 1)
            for c in range(n_col):
                if c < n_col - 1:
                    nxt = jnp.where(lane16 < LANE - 1, left[c], left[c + 1])
                else:
                    nxt = jnp.where(lane16 < tail - 1, left[c], first_to_end)
                prv = jnp.where(lane16 > 0, right[c], right[c - 1] if c > 0 else end_to_first)
                value = (
                    (nxt - prv) - east_f[c, part(above), :] * c_above + east_f[c, part(below), :] * c_below
                ) * weight
                if c == n_col - 1:
                    value = jnp.where(lane16 < tail, value, 0.0)
                field[j, pl.ds(g * 16, 16), c * LANE : (c + 1) * LANE] = value.astype(BF16)
            return carry

        lax.fori_loop(0, padded // 16, group, 0)
        sketch[j] = dot(signs, field[j])

    def take_halo():
        for side in (0, 1):
            edges[1 - side].wait_recv()
            for c in range(n_col):
                east_f[c, pl.ds(padded * rows + side, padded, stride=rows), :] = edge_recv[
                    side, :, c * LANE : (c + 1) * LANE
                ].astype(F32)

    hops = n_tm // 2
    halves = (range(0, NSUB // 2), range(NSUB // 2, NSUB))

    def cols(h):
        return pl.ds(h * piece, piece)

    def row_at(offset):
        return lax.rem(m + n_tm + offset, n_tm)

    def when_class(j, edge, run):
        is_edge = jnp.logical_or(j == 0, j == rows - 1)
        pl.when(is_edge if edge else jnp.logical_not(is_edge))(run)

    def chain(side, k, h):
        return remote(
            chain_send.at[side, k, :, cols(h)],
            chain_recv.at[side, k, :, cols(h)],
            chain_ssem.at[side, k, h],
            chain_rsem.at[side, k, h],
            (z_minus, z_plus)[side],
        )

    def chain_row(side, k):
        return row_at(hops + k) if side == 0 else row_at(hops - k)

    def begin(k, edge):
        for side in (0, 1):
            j = chain_row(side, k)

            def run(side=side, j=j):
                compute_row(j)
                if k > 1:
                    return
                for other in (0, 1):
                    if k == 1 and other == side:
                        continue
                    for h in halves[other]:
                        target = side if k == 1 else other
                        chain_send[target, k, :, cols(h)] = sketch[j, :, cols(h)].astype(BF16)
                        chain(target, k, h).start()

            if k > 0 or side == 0:
                when_class(j, edge, run)

    def relay(k, edge):
        for side in (0, 1):
            j = chain_row(side, k)

            def run(side=side, j=j):
                for h in halves[side] if k == 1 else range(NSUB):
                    chain(side, k - 1, h).wait_recv()
                    value = sketch[j, :, cols(h)] + chain_recv[side, k - 1, :, cols(h)].astype(F32)
                    chain_send[side, k, :, cols(h)] = value.astype(BF16)
                    chain(side, k, h).start()

            when_class(j, edge, run)

    def gather(side, k, h, j):
        return remote(
            whole.at[j, :, cols(h)],
            whole.at[j, :, cols(h)],
            gather_ssem.at[side, k, h],
            gather_rsem.at[side, k, h],
            (z_minus, z_plus)[side],
        )

    def consume(j):
        value = whole[j]
        mine[0:RANK, :] += dot_t(value, field[j])
        grams[j] = dot_t(value, value)

    def finish(edge):
        def run():
            for h in range(NSUB):
                value = sketch[m, :, cols(h)]
                for side in (0, 1):
                    chain(side, hops - 1, h).wait_recv()
                    value = value + chain_recv[side, hops - 1, :, cols(h)].astype(F32)
                whole[m, :, cols(h)] = value.astype(BF16)
                for side in (0, 1):
                    gather(side, 0, h, m).start()
            consume(m)

        when_class(m, edge, run)

    def spread(k, edge):
        for side in (0, 1):
            j = row_at(k) if side == 0 else row_at(-k)

            def run(side=side, j=j):
                for h in range(NSUB):
                    gather(side, k - 1, h, j).wait_recv()
                    if k < hops - 1 or h in halves[side]:
                        gather(side, k, h, j).start()
                consume(j)

            when_class(j, edge, run)

    def last(edge):
        j = row_at(hops)

        def run():
            for side in (0, 1):
                for h in halves[side]:
                    gather(side, hops - 1, h, j).wait_recv()
            consume(j)

        when_class(j, edge, run)

    mine[...] = jnp.zeros(mine.shape, F32)
    begin(0, False)
    begin(1, False)
    relay(1, False)
    take_halo()
    begin(0, True)
    begin(2, False)
    begin(1, True)
    relay(2, False)
    relay(1, True)
    begin(3, False)
    begin(2, True)
    relay(3, False)
    relay(2, True)
    begin(3, True)
    compute_row(m)
    relay(3, True)
    finish(False)
    finish(True)
    for k in range(1, hops + 1):
        if k < hops:
            spread(k, False)
        else:
            last(False)
        if k == 1:
            continue
        spread(k - 1, True)
    last(True)

    gram = grams[0]
    for j in range(1, rows):
        gram = gram + grams[j]
    mine[RANK : 2 * RANK, 0:RANK] = gram

    pair = remote(mine, pair_recv, pair_sem.at[0], pair_sem.at[1], partner)
    pair.start()
    pair.wait_recv()
    value = mine[...] + pair_recv[...]
    for store, ssem, rsem, count, here, peer_of in (
        (x_slots, x_ssem, x_rsem, n_x, x, x_peer),
        (y_slots, y_ssem, y_rsem, n_y, y, y_peer),
    ):
        store[here] = value
        for d in range(1, count):
            remote(store.at[here], store.at[here], ssem.at[d - 1], rsem.at[d - 1], peer_of(d)).start()
        for d in range(1, count):
            origin = lax.rem(here + count - d, count)
            remote(store.at[origin], store.at[origin], ssem.at[d - 1], rsem.at[d - 1], peer_of(d)).wait_recv()
        value = store[0]
        for i in range(1, count):
            value = value + store[i]

    projected = value[0:RANK, :]
    inverse = inverse_factor(value[RANK : 2 * RANK, :] * (1.0 / cells))
    coeffs = dot(inverse, projected, HIGHEST) * (1.0 / cells)
    coeffs = jnp.where(iota((RANK, padded), 1) < count_ref[0], coeffs, 0.0)
    coeffs_ref[...] = coeffs[:, :slots]

    size = RANK * rows
    take_row = (iota((size, RANK), 0) // rows == iota((size, RANK), 1)).astype(F32).astype(BF16)
    take_col = (iota((RANK, size), 0) == lax.rem(iota((RANK, size), 1), RANK)).astype(F32).astype(BF16)
    same = lax.rem(iota((size, size), 0), rows) == iota((size, size), 1) // RANK
    flat = whole[...].reshape(size, width)
    basis = None
    for half in split(inverse):
        spread = dot(take_row, half).astype(BF16)
        spread = dot(spread, take_col)
        spread = jnp.where(same, spread, 0.0).astype(BF16)
        term = dot(spread, flat)
        basis = term if basis is None else basis + term
    basis_ref[...] = basis.reshape(RANK, rows, width)[:, :, :lons].astype(BF16)

    for copy in edges:
        copy.wait_send()
    for side in (0, 1):
        for k in range(hops):
            for h in range(NSUB):
                if k > 0 or h in halves[side]:
                    chain(side, k, h).wait_send()
                if k < hops - 1 or h in halves[side]:
                    gather(side, k, h, m).wait_send()
    pair.wait_send()
    for store, ssem, rsem, count, here, peer_of in (
        (x_slots, x_ssem, x_rsem, n_x, x, x_peer),
        (y_slots, y_ssem, y_rsem, n_y, y, y_peer),
    ):
        for d in range(1, count):
            remote(store.at[here], store.at[here], ssem.at[d - 1], rsem.at[d - 1], peer_of(d)).wait_send()


def local(n_tm, n_lat, n_x, wind_east, wind_north, snap_counts, snap_ids):
    slots, rows, lons = wind_east.shape
    padded = -(-slots // LANE) * LANE
    n_col = -(-lons // LANE)
    width = n_col * LANE
    n_y = n_lat // (2 * n_x)
    ids = jnp.pad(snap_ids, (0, padded - slots)).reshape(1, padded)
    shape = (slots, rows, lons, n_tm, n_lat, n_x)
    hops = n_tm // 2
    dma = pltpu.SemaphoreType.DMA
    return pl.pallas_call(
        functools.partial(kernel, shape),
        out_shape=(
            jax.ShapeDtypeStruct((RANK, rows, lons), BF16),
            jax.ShapeDtypeStruct((RANK, slots), F32),
        ),
        in_specs=[
            pl.BlockSpec(memory_space=pl.ANY),
            pl.BlockSpec(memory_space=pl.ANY),
            pl.BlockSpec(memory_space=pltpu.SMEM),
            pl.BlockSpec(memory_space=pltpu.VMEM),
        ],
        out_specs=(pl.BlockSpec(memory_space=pltpu.VMEM), pl.BlockSpec(memory_space=pltpu.VMEM)),
        scratch_shapes=[
            pltpu.VMEM((slots, rows, lons), BF16),
            pltpu.VMEM((slots, rows, lons), BF16),
            pltpu.VMEM((n_col, 2 * padded * rows, LANE), F32),
            pltpu.VMEM((n_col, padded * rows, LANE), F32),
            pltpu.VMEM((2, padded, width), BF16),
            pltpu.VMEM((2, padded, width), BF16),
            pltpu.VMEM((rows, padded, width), BF16),
            pltpu.VMEM((rows, RANK, width), F32),
            pltpu.VMEM((2, 16, LANE), F32),
            pltpu.VMEM((2, hops, RANK, width), BF16),
            pltpu.VMEM((2, hops, RANK, width), BF16),
            pltpu.VMEM((rows, RANK, width), BF16),
            pltpu.VMEM((rows, RANK, RANK), F32),
            pltpu.VMEM((2 * RANK, LANE), F32),
            pltpu.VMEM((2 * RANK, LANE), F32),
            pltpu.VMEM((n_x, 2 * RANK, LANE), F32),
            pltpu.VMEM((n_y, 2 * RANK, LANE), F32),
            dma((2, NLOAD)),
            dma((2,)),
            dma((2,)),
            dma((2, hops, NSUB)),
            dma((2, hops, NSUB)),
            dma((2, hops, NSUB)),
            dma((2, hops, NSUB)),
            dma((2,)),
            dma((n_x - 1,)),
            dma((n_x - 1,)),
            dma((n_y - 1,)),
            dma((n_y - 1,)),
        ],
        compiler_params=pltpu.CompilerParams(
            collective_id=0, has_side_effects=True, vmem_limit_bytes=60 * 1024 * 1024
        ),
        name="eof",
    )(wind_east, wind_north, snap_counts, ids)


def solution(mesh):
    in_specs = (P("tm", "lat", None), P("tm", "lat", None), P("tm"), P("tm"))
    out_specs = (P(None, "lat", None), P(None, "tm"))
    body = functools.partial(local, mesh.shape["tm"], mesh.shape["lat"], 4)
    return jax.shard_map(body, mesh=mesh, in_specs=in_specs, out_specs=out_specs, check_vma=False)
```

```python
import functools

import jax
import jax.numpy as jnp
import numpy as np
from jax import lax
from jax.experimental import pallas as pl
from jax.experimental.pallas import tpu as pltpu
from jax.sharding import PartitionSpec as P

RANK = 32
LANE = 128
F32 = jnp.float32
BF16 = jnp.bfloat16
MESH = pl.DeviceIdType.MESH
HIGHEST = lax.Precision.HIGHEST
NSUB = 4


def dot(a, b, precision=None):
    return lax.dot_general(
        a, b, (((1,), (0,)), ((), ())), precision=precision, preferred_element_type=F32
    )


def dot_t(a, b, precision=None):
    return lax.dot_general(
        a, b, (((1,), (1,)), ((), ())), precision=precision, preferred_element_type=F32
    )


def iota(shape, dim):
    return lax.broadcasted_iota(jnp.int32, shape, dim)


def split(x):
    high = x.astype(BF16)
    return high, (x - high.astype(F32)).astype(BF16)


def cosine(x):
    y = x * x
    p = jnp.full_like(y, -1.0 / 3628800.0)
    for coefficient in (1.0 / 40320.0, -1.0 / 720.0, 1.0 / 24.0, -0.5, 1.0):
        p = p * y + coefficient
    return p


def inverse_factor(gram):
    row, lane = iota((RANK, LANE), 0), iota((RANK, LANE), 1)
    a = jnp.where(lane == row + RANK, 1.0, gram)
    for k in range(RANK - 1):
        pivot_row = a[k : k + 1, :]
        column = a[:, k : k + 1]
        factor = column / a[k : k + 1, k : k + 1]
        a = a - jnp.where(row > k, factor * pivot_row, 0.0)
    diagonal = jnp.sum(jnp.where(row == lane, a, 0.0), axis=1, keepdims=True)
    scaled = a * lax.rsqrt(diagonal)
    return pltpu.roll(scaled, LANE - RANK, 1)[:, :RANK]


def kernel(
    shape,
    east_hbm,
    north_hbm,
    count_ref,
    ids_ref,
    basis_ref,
    coeffs_ref,
    east_f,
    north_f,
    east_b,
    north_b,
    spread_signs,
    east_sketch,
    north_sketch,
    sketch,
    halo_send,
    halo_recv,
    edge_send,
    edge_recv,
    field,
    chain_send,
    chain_recv,
    whole,
    projection,
    gram_part,
    gram_slots,
    x_slots,
    y_slots,
    load_sem,
    halo_ssem,
    halo_rsem,
    edge_ssem,
    edge_rsem,
    chain_ssem,
    chain_rsem,
    gather_ssem,
    gather_rsem,
    gram_ssem,
    gram_rsem,
    x_ssem,
    x_rsem,
    y_ssem,
    y_rsem,
):
    slots, rows, lons, n_tm, n_lat, n_x = shape
    n_y = n_lat // (2 * n_x)
    n_col = pl.cdiv(lons, LANE)
    tail = lons - (n_col - 1) * LANE
    padded = field.shape[1]
    width = n_col * LANE
    piece = width // NSUB
    total_rows = rows * n_lat
    cells = total_rows * lons

    m = lax.axis_index("tm")
    b = lax.axis_index("lat")
    core = lax.rem(b, 2)
    x = lax.rem(b // 2, n_x)
    y = b // (2 * n_x)
    south, north = {"lat": lax.rem(b + 1, n_lat)}, {"lat": lax.rem(b + n_lat - 1, n_lat)}

    def z_at(d):
        return {"tm": lax.rem(m + n_tm + d, n_tm)}

    def x_peer(i, sign=1):
        dx, flip = i // 2, i % 2
        other = core + flip - 2 * flip * core
        return lax.rem(x + n_x + sign * dx, n_x) * 2 + other

    def y_peer(d, sign=1):
        return lax.rem(y + n_y + sign * d, n_y)

    x_line = [{"lat": y * (2 * n_x) + x_peer(i)} for i in range(1, 2 * n_x)]
    y_line = [{"lat": y_peer(d) * (2 * n_x) + x * 2 + core} for d in range(1, n_y)]
    peers = [z_at(d) for d in (-2, -1, 1, 2)] + [south, north] + x_line + y_line
    barrier = pltpu.get_barrier_semaphore()
    for peer in peers:
        pl.semaphore_signal(barrier, inc=1, device_id=peer, device_id_type=MESH)

    def remote(src, dst, ssem, rsem, peer):
        return pltpu.make_async_remote_copy(
            src_ref=src, dst_ref=dst, send_sem=ssem, recv_sem=rsem, device_id=peer, device_id_type=MESH
        )

    loads = [
        pltpu.make_async_copy(east_hbm, east_b, load_sem.at[0]),
        pltpu.make_async_copy(north_hbm, north_b, load_sem.at[1]),
    ]
    for copy in loads:
        copy.start()

    ids = jnp.broadcast_to(ids_ref[...], (RANK, slots))
    column = iota((RANK, slots), 0)
    mixed = ids * 1103515245 + column * 40503 + 12345
    mixed = jnp.bitwise_xor(mixed, jnp.right_shift(mixed, 13))
    mixed = mixed * 1664525 + 1013904223
    mixed = jnp.bitwise_xor(mixed, jnp.right_shift(mixed, 16))
    flipped = jnp.bitwise_and(jnp.right_shift(mixed, 7), 1)
    slot_used = iota((RANK, slots), 1) < count_ref[0]
    signs = jnp.where(slot_used, (1 - 2 * flipped).astype(F32), 0.0).astype(BF16)
    depth = slots * rows
    repeat = (iota((slots, depth), 1) // rows == iota((slots, depth), 0)).astype(F32).astype(BF16)
    repeated = dot(signs, repeat)
    lane_row = lax.rem(iota((RANK, depth), 1), rows)
    for j in range(rows):
        spread_signs[j * RANK : (j + 1) * RANK, :] = jnp.where(lane_row == j, repeated, 0.0).astype(BF16)

    band_row = iota((16, LANE), 0) + (b * rows - 1)
    cosines = cosine((total_rows // 2 - band_row).astype(F32) * (jnp.pi / 720.0))
    weights = 0.5 / jnp.sqrt(cosines)
    inside = jnp.logical_and(band_row >= 0, band_row < total_rows)
    cosines = jnp.where(inside, cosines, 0.0)

    for wide in (east_f, north_f):
        wide[:, depth:, :] = jnp.zeros((n_col, padded * rows - depth, LANE), F32)

    loads[0].wait()
    east_sketch[1 : rows + 1, :, 0:lons] = dot(spread_signs[...], east_b[...]).reshape(rows, RANK, lons)
    for side, j in ((0, 1), (1, rows)):
        halo_send[side] = east_sketch[j].astype(BF16)
    pl.semaphore_wait(barrier, len(peers))
    halos = [
        remote(halo_send.at[0], halo_recv.at[1], halo_ssem.at[0], halo_rsem.at[1], north),
        remote(halo_send.at[1], halo_recv.at[0], halo_ssem.at[1], halo_rsem.at[0], south),
    ]
    for copy in halos:
        copy.start()
    loads[1].wait()
    north_sketch[:, :, 0:lons] = dot(spread_signs[...], north_b[...]).reshape(rows, RANK, lons)

    def roll_pair(tiles, lane):
        left = [pltpu.roll(t, LANE - 1, 1) for t in tiles]
        right = [pltpu.roll(t, 1, 1) for t in tiles]
        first_to_end = pltpu.roll(tiles[0], tail - 1, 1)
        end_to_first = pltpu.roll(tiles[-1], LANE - tail + 1, 1)
        result = []
        for c in range(n_col):
            if c < n_col - 1:
                nxt = jnp.where(lane < LANE - 1, left[c], left[c + 1])
            else:
                nxt = jnp.where(lane < tail - 1, left[c], first_to_end)
            prv = jnp.where(lane > 0, right[c], right[c - 1] if c > 0 else end_to_first)
            result.append(nxt - prv)
        return result

    def constants(j, count):
        def spread(t, i):
            return jnp.broadcast_to(t[i : i + 1, :], (count, LANE))

        return spread(cosines, j), spread(cosines, j + 2), spread(weights, j + 1)

    lane32 = iota((RANK, LANE), 1)

    def sketch_row(j):
        c_above, c_below, weight = constants(j, RANK)
        zonal = roll_pair([north_sketch[j, :, c * LANE : (c + 1) * LANE] for c in range(n_col)], lane32)
        for c in range(n_col):
            part = slice(c * LANE, (c + 1) * LANE)
            value = (zonal[c] - east_sketch[j, :, part] * c_above + east_sketch[j + 2, :, part] * c_below) * weight
            if c == n_col - 1:
                value = jnp.where(lane32 < tail, value, 0.0)
            sketch[j, :, part] = value

    lane16 = iota((16, LANE), 1)

    def field_row(j, east_above, east_below):
        c_above, c_below, weight = constants(j, 16)

        def group(g, carry):
            part = pl.ds(g * (16 * rows) + j, 16, stride=rows)
            zonal = roll_pair([north_f[c, part, :] for c in range(n_col)], lane16)
            for c in range(n_col):
                value = (zonal[c] - east_above(g, c) * c_above + east_below(g, c) * c_below) * weight
                if c == n_col - 1:
                    value = jnp.where(lane16 < tail, value, 0.0)
                field[j, pl.ds(g * 16, 16), c * LANE : (c + 1) * LANE] = value.astype(BF16)
            return carry

        lax.fori_loop(0, padded // 16, group, 0)

    def local_east(j):
        return lambda g, c: east_f[c, pl.ds(g * (16 * rows) + j, 16, stride=rows), :]

    def halo_east(side):
        return lambda g, c: edge_recv[side, pl.ds(g * 16, 16), c * LANE : (c + 1) * LANE].astype(F32)

    def widen(flat, wide):
        def run():
            for c in range(n_col):
                w = LANE if c < n_col - 1 else tail
                wide[c, 0:depth, 0:w] = flat[:, c * LANE : c * LANE + w].astype(F32)

        return run

    def send_edges():
        for side, j in ((0, 0), (1, rows - 1)):
            for c in range(n_col):
                edge_send[side, :, c * LANE : (c + 1) * LANE] = east_f[
                    c, pl.ds(j, padded, stride=rows), :
                ].astype(BF16)
        for copy in edges:
            copy.start()

    edges = [
        remote(edge_send.at[0], edge_recv.at[1], edge_ssem.at[0], edge_rsem.at[1], north),
        remote(edge_send.at[1], edge_recv.at[0], edge_ssem.at[1], edge_rsem.at[0], south),
    ]

    def field_task(j):
        if 0 < j < rows - 1:
            return lambda: field_row(j, local_east(j - 1), local_east(j + 1))
        if j == 0:
            def run():
                edges[1].wait_recv()
                field_row(0, halo_east(0), local_east(1))
        else:
            def run():
                edges[0].wait_recv()
                field_row(j, local_east(j - 1), halo_east(1))
        return run

    tasks = [widen(east_b, east_f), send_edges, widen(north_b, north_f)]
    tasks += [field_task(j) for j in list(range(1, rows - 1)) + [0, rows - 1]]

    def work(count):
        for _ in range(min(count, len(tasks))):
            tasks.pop(0)()

    far, mid, near, summed = range(4)
    reach = (4, 3, 1, 2)
    route = (2, 1, 1, 2)
    toward = (-1, 1)
    halves = (list(range(0, NSUB // 2)), list(range(NSUB // 2, NSUB)))
    pieces = (halves[1] + halves[0], halves[0] + halves[1])

    def cols(h):
        return pl.ds(h * piece, piece)

    def row_at(offset):
        return lax.rem(m + n_tm + offset, n_tm)

    def chain(side, kind, h):
        return remote(
            chain_send.at[side, kind, :, cols(h)],
            chain_recv.at[side, kind, :, cols(h)],
            chain_ssem.at[side, kind, h],
            chain_rsem.at[side, kind, h],
            z_at(toward[side] * route[kind]),
        )

    def begin(kind, edge):
        for side in (0, 1):
            j = row_at(toward[side] * reach[kind])

            def run(side=side, j=j):
                for h in halves[side] if kind == far else pieces[side]:
                    chain_send[side, kind, :, cols(h)] = sketch[j, :, cols(h)].astype(BF16)
                    chain(side, kind, h).start()

            is_edge = jnp.logical_or(j == 0, j == rows - 1)
            pl.when(is_edge if edge else jnp.logical_not(is_edge))(run)

    def relay(side):
        j = row_at(toward[side] * 2)
        for h in pieces[side]:
            value = sketch[j, :, cols(h)]
            for kind in (mid, far) if h in halves[side] else (mid,):
                chain(side, kind, h).wait_recv()
                value = value + chain_recv[side, kind, :, cols(h)].astype(F32)
            chain_send[side, summed, :, cols(h)] = value.astype(BF16)
            chain(side, summed, h).start()

    to_one, to_two, to_three, to_four = range(4)
    stride_of = (1, 2, 1, 2)

    def gather(side, kind, h, j):
        return remote(
            whole.at[j, :, cols(h)],
            whole.at[j, :, cols(h)],
            gather_ssem.at[side, kind, h],
            gather_rsem.at[side, kind, h],
            z_at(toward[side] * stride_of[kind]),
        )

    def arrive(side, kind):
        j = row_at(-toward[side] * (kind + 1))
        for h in halves[side] if kind == to_four else pieces[side]:
            gather(side, kind, h, j).wait_recv()
            if kind == to_two:
                if h in halves[side]:
                    gather(side, to_four, h, j).start()
                gather(side, to_three, h, j).start()

    def consume(j):
        projection[...] += dot_t(whole[j], field[j])

    class LatSum:
        def __init__(self, n):
            self.levels = (
                (x_slots.at[n], x_ssem.at[n], x_rsem.at[n], x * 2 + core, x_line, x_peer),
                (y_slots.at[n], y_ssem.at[n], y_rsem.at[n], y, y_line, y_peer),
            )

        def copy(self, level, i, slot):
            slots_of, ssem, rsem, _, line, _ = self.levels[level]
            return remote(slots_of.at[slot], slots_of.at[slot], ssem.at[i], rsem.at[i], line[i])

        def send(self, level, value):
            slots_of, _, _, here, line, _ = self.levels[level]
            slots_of[here] = value
            for i in range(len(line)):
                self.copy(level, i, here).start()

        def total(self, level):
            slots_of, _, _, _, line, peer_of = self.levels[level]
            for i in range(len(line)):
                self.copy(level, i, peer_of(i + 1, -1)).wait_recv()
            value = slots_of[0]
            for i in range(1, len(line) + 1):
                value = value + slots_of[i]
            return value

        def drain(self):
            for level, (_, _, _, here, line, _) in enumerate(self.levels):
                for i in range(len(line)):
                    self.copy(level, i, here).wait_send()

    def gram_copy(d, slot):
        return remote(
            gram_slots.at[slot], gram_slots.at[slot], gram_ssem.at[d - 1], gram_rsem.at[d - 1],
            {"tm": lax.rem(m + d, n_tm)},
        )

    gram_sum, projection_sum = LatSum(0), LatSum(1)
    projection[...] = jnp.zeros(projection.shape, F32)

    for j in range(1, rows - 1):
        sketch_row(j)
    for kind in (far, mid, near):
        begin(kind, False)
    for side in (0, 1):
        halos[1 - side].wait_recv()
        east_sketch[side * (rows + 1)] = halo_recv[side].astype(F32)
    for j in (0, rows - 1):
        sketch_row(j)
    for kind in (far, mid, near):
        begin(kind, True)
    work(3)
    relay(0)
    relay(1)
    work(3)
    for h in range(NSUB):
        value = sketch[m, :, cols(h)]
        for kind in (near, summed):
            for side in (0, 1):
                chain(side, kind, h).wait_recv()
                value = value + chain_recv[side, kind, :, cols(h)].astype(F32)
        whole[m, :, cols(h)] = value.astype(BF16)
        for kind in (to_two, to_one):
            for side in (0, 1):
                gather(side, kind, h, m).start()
    own = whole[m]
    gram_part[...] = jnp.zeros((RANK, LANE), F32)
    gram_part[:, 0:RANK] = dot_t(own, own)
    gram_sum.send(0, gram_part[...])
    work(2)
    arrive(0, to_two)
    arrive(1, to_two)
    gram_sum.send(1, gram_sum.total(0))
    work(len(tasks))
    for offset in (0, -2, 2):
        consume(row_at(offset))
    gram_slots[m] = gram_sum.total(1)
    for d in range(1, n_tm):
        gram_copy(d, m).start()
    for kind, offset in ((to_one, 1), (to_three, 3)):
        for side in (0, 1):
            arrive(side, kind)
            consume(row_at(-toward[side] * offset))
    arrive(0, to_four)
    arrive(1, to_four)
    consume(row_at(4))
    projection_sum.send(0, projection[...])
    for d in range(1, n_tm):
        gram_copy(d, lax.rem(m + n_tm - d, n_tm)).wait_recv()
    gram = gram_slots[0]
    for i in range(1, n_tm):
        gram = gram + gram_slots[i]
    inverse = inverse_factor(gram * (1.0 / cells))
    projection_sum.send(1, projection_sum.total(0))

    size = RANK * rows
    take_row = (iota((size, RANK), 0) // rows == iota((size, RANK), 1)).astype(F32).astype(BF16)
    take_col = (iota((RANK, size), 0) == lax.rem(iota((RANK, size), 1), RANK)).astype(F32).astype(BF16)
    same = lax.rem(iota((size, size), 0), rows) == iota((size, size), 1) // RANK
    flat = whole[...].reshape(size, width)
    basis = None
    for half in split(inverse):
        spread = dot(take_row, half).astype(BF16)
        spread = dot(spread, take_col)
        spread = jnp.where(same, spread, 0.0).astype(BF16)
        term = dot(spread, flat)
        basis = term if basis is None else basis + term
    basis_ref[...] = basis.reshape(RANK, rows, width)[:, :, :lons].astype(BF16)
    projected = projection_sum.total(1)
    coeffs = dot(inverse, projected, HIGHEST) * (1.0 / cells)
    coeffs = jnp.where(iota((RANK, padded), 1) < count_ref[0], coeffs, 0.0)
    coeffs_ref[...] = coeffs[:, :slots]

    for copy in halos + edges:
        copy.wait_send()
    for side in (0, 1):
        for kind in range(4):
            for h in range(NSUB):
                if kind != far or h in halves[side]:
                    chain(side, kind, h).wait_send()
                if kind != to_four or h in halves[side]:
                    gather(side, kind, h, m).wait_send()
    for part in (gram_sum, projection_sum):
        part.drain()
    for d in range(1, n_tm):
        gram_copy(d, m).wait_send()


def local(n_tm, n_lat, n_x, wind_east, wind_north, snap_counts, snap_ids):
    slots, rows, lons = wind_east.shape
    padded = -(-slots // LANE) * LANE
    n_col = -(-lons // LANE)
    width = n_col * LANE
    n_y = n_lat // (2 * n_x)
    ids = snap_ids.reshape(1, slots)
    shape = (slots, rows, lons, n_tm, n_lat, n_x)
    dma = pltpu.SemaphoreType.DMA
    return pl.pallas_call(
        functools.partial(kernel, shape),
        out_shape=(
            jax.ShapeDtypeStruct((RANK, rows, lons), BF16),
            jax.ShapeDtypeStruct((RANK, slots), F32),
        ),
        in_specs=[
            pl.BlockSpec(memory_space=pl.ANY),
            pl.BlockSpec(memory_space=pl.ANY),
            pl.BlockSpec(memory_space=pltpu.SMEM),
            pl.BlockSpec(memory_space=pltpu.VMEM),
        ],
        out_specs=(pl.BlockSpec(memory_space=pltpu.VMEM), pl.BlockSpec(memory_space=pltpu.VMEM)),
        scratch_shapes=[
            pltpu.VMEM((n_col, padded * rows, LANE), F32),
            pltpu.VMEM((n_col, padded * rows, LANE), F32),
            pltpu.VMEM((slots * rows, lons), BF16),
            pltpu.VMEM((slots * rows, lons), BF16),
            pltpu.VMEM((rows * RANK, slots * rows), BF16),
            pltpu.VMEM((rows + 2, RANK, width), F32),
            pltpu.VMEM((rows, RANK, width), F32),
            pltpu.VMEM((rows, RANK, width), F32),
            pltpu.VMEM((2, RANK, width), BF16),
            pltpu.VMEM((2, RANK, width), BF16),
            pltpu.VMEM((2, padded, width), BF16),
            pltpu.VMEM((2, padded, width), BF16),
            pltpu.VMEM((rows, padded, width), BF16),
            pltpu.VMEM((2, 4, RANK, width), BF16),
            pltpu.VMEM((2, 4, RANK, width), BF16),
            pltpu.VMEM((rows, RANK, width), BF16),
            pltpu.VMEM((RANK, padded), F32),
            pltpu.VMEM((RANK, LANE), F32),
            pltpu.VMEM((n_tm, RANK, LANE), F32),
            pltpu.VMEM((2, 2 * n_x, RANK, LANE), F32),
            pltpu.VMEM((2, n_y, RANK, LANE), F32),
            dma((2,)),
            dma((2,)),
            dma((2,)),
            dma((2,)),
            dma((2,)),
            dma((2, 4, NSUB)),
            dma((2, 4, NSUB)),
            dma((2, 4, NSUB)),
            dma((2, 4, NSUB)),
            dma((n_tm - 1,)),
            dma((n_tm - 1,)),
            dma((2, 2 * n_x - 1)),
            dma((2, 2 * n_x - 1)),
            dma((2, n_y - 1)),
            dma((2, n_y - 1)),
        ],
        compiler_params=pltpu.CompilerParams(
            collective_id=0, has_side_effects=True, vmem_limit_bytes=60 * 1024 * 1024
        ),
        name="eof",
    )(
        wind_east.reshape(slots * rows, lons), wind_north.reshape(slots * rows, lons), snap_counts, ids
    )


def solution(mesh):
    in_specs = (P("tm", "lat", None), P("tm", "lat", None), P("tm"), P("tm"))
    out_specs = (P(None, "lat", None), P(None, "tm"))
    body = functools.partial(local, mesh.shape["tm"], mesh.shape["lat"], 4)
    return jax.shard_map(body, mesh=mesh, in_specs=in_specs, out_specs=out_specs, check_vma=False)
```

```python
import functools

import jax
import jax.numpy as jnp
import numpy as np
from jax import lax
from jax.experimental import pallas as pl
from jax.experimental.pallas import tpu as pltpu
from jax.sharding import PartitionSpec as P

RANK = 32
LANE = 128
F32 = jnp.float32
BF16 = jnp.bfloat16
MESH = pl.DeviceIdType.MESH
HIGHEST = lax.Precision.HIGHEST
NSUB = 4


def dot(a, b, precision=None):
    return lax.dot_general(
        a, b, (((1,), (0,)), ((), ())), precision=precision, preferred_element_type=F32
    )


def dot_t(a, b, precision=None):
    return lax.dot_general(
        a, b, (((1,), (1,)), ((), ())), precision=precision, preferred_element_type=F32
    )


def iota(shape, dim):
    return lax.broadcasted_iota(jnp.int32, shape, dim)


def split(x):
    high = x.astype(BF16)
    return high, (x - high.astype(F32)).astype(BF16)


def cosine(x):
    y = x * x
    p = jnp.full_like(y, -1.0 / 3628800.0)
    for coefficient in (1.0 / 40320.0, -1.0 / 720.0, 1.0 / 24.0, -0.5, 1.0):
        p = p * y + coefficient
    return p


def inverse_factor(gram):
    row, lane = iota((RANK, LANE), 0), iota((RANK, LANE), 1)
    a = jnp.where(lane == row + RANK, 1.0, gram)
    for k in range(RANK - 1):
        pivot_row = a[k : k + 1, :]
        column = a[:, k : k + 1]
        factor = column / a[k : k + 1, k : k + 1]
        a = a - jnp.where(row > k, factor * pivot_row, 0.0)
    diagonal = jnp.sum(jnp.where(row == lane, a, 0.0), axis=1, keepdims=True)
    scaled = a * lax.rsqrt(diagonal)
    return pltpu.roll(scaled, LANE - RANK, 1)[:, :RANK]


def kernel(
    shape,
    east_hbm,
    north_hbm,
    count_ref,
    ids_ref,
    basis_ref,
    coeffs_ref,
    east_f,
    north_f,
    east_b,
    north_b,
    spread_signs,
    east_sketch,
    north_sketch,
    sketch,
    halo_send,
    halo_recv,
    edge_send,
    edge_recv,
    field,
    chain_send,
    chain_recv,
    whole,
    projection,
    gram_part,
    gram_slots,
    x_slots,
    y_slots,
    load_sem,
    halo_ssem,
    halo_rsem,
    edge_ssem,
    edge_rsem,
    chain_ssem,
    chain_rsem,
    gather_ssem,
    gather_rsem,
    gram_ssem,
    gram_rsem,
    x_ssem,
    x_rsem,
    y_ssem,
    y_rsem,
):
    slots, rows, lons, n_tm, n_lat, n_x = shape
    n_y = n_lat // (2 * n_x)
    n_col = pl.cdiv(lons, LANE)
    tail = lons - (n_col - 1) * LANE
    padded = field.shape[1]
    width = n_col * LANE
    piece = width // NSUB
    total_rows = rows * n_lat
    cells = total_rows * lons

    m = lax.axis_index("tm")
    b = lax.axis_index("lat")
    core = lax.rem(b, 2)
    x = lax.rem(b // 2, n_x)
    y = b // (2 * n_x)
    south, north = {"lat": lax.rem(b + 1, n_lat)}, {"lat": lax.rem(b + n_lat - 1, n_lat)}

    def z_at(d):
        return {"tm": lax.rem(m + n_tm + d, n_tm)}

    def x_peer(i, sign=1):
        dx, flip = i // 2, i % 2
        other = core + flip - 2 * flip * core
        return lax.rem(x + n_x + sign * dx, n_x) * 2 + other

    def y_peer(d, sign=1):
        return lax.rem(y + n_y + sign * d, n_y)

    x_line = [{"lat": y * (2 * n_x) + x_peer(i)} for i in range(1, 2 * n_x)]
    y_line = [{"lat": y_peer(d) * (2 * n_x) + x * 2 + core} for d in range(1, n_y)]
    peers = [z_at(d) for d in (-2, -1, 1, 2)] + [south, north] + x_line + y_line
    barrier = pltpu.get_barrier_semaphore()
    for peer in peers:
        pl.semaphore_signal(barrier, inc=1, device_id=peer, device_id_type=MESH)

    def remote(src, dst, ssem, rsem, peer):
        return pltpu.make_async_remote_copy(
            src_ref=src, dst_ref=dst, send_sem=ssem, recv_sem=rsem, device_id=peer, device_id_type=MESH
        )

    loads = [
        pltpu.make_async_copy(east_hbm, east_b, load_sem.at[0]),
        pltpu.make_async_copy(north_hbm, north_b, load_sem.at[1]),
    ]
    for copy in loads:
        copy.start()

    ids = jnp.broadcast_to(ids_ref[...], (RANK, slots))
    column = iota((RANK, slots), 0)
    mixed = ids * 1103515245 + column * 40503 + 12345
    mixed = jnp.bitwise_xor(mixed, jnp.right_shift(mixed, 13))
    mixed = mixed * 1664525 + 1013904223
    mixed = jnp.bitwise_xor(mixed, jnp.right_shift(mixed, 16))
    flipped = jnp.bitwise_and(jnp.right_shift(mixed, 7), 1)
    slot_used = iota((RANK, slots), 1) < count_ref[0]
    signs = jnp.where(slot_used, (1 - 2 * flipped).astype(F32), 0.0).astype(BF16)
    depth = slots * rows
    repeat = (iota((slots, depth), 1) // rows == iota((slots, depth), 0)).astype(F32).astype(BF16)
    repeated = dot(signs, repeat)
    lane_row = lax.rem(iota((RANK, depth), 1), rows)
    for j in range(rows):
        spread_signs[j * RANK : (j + 1) * RANK, :] = jnp.where(lane_row == j, repeated, 0.0).astype(BF16)

    band_row = iota((16, LANE), 0) + (b * rows - 1)
    cosines = cosine((total_rows // 2 - band_row).astype(F32) * (jnp.pi / 720.0))
    weights = 0.5 / jnp.sqrt(cosines)
    inside = jnp.logical_and(band_row >= 0, band_row < total_rows)
    cosines = jnp.where(inside, cosines, 0.0)

    for wide in (east_f, north_f):
        wide[:, depth:, :] = jnp.zeros((n_col, padded * rows - depth, LANE), F32)

    loads[0].wait()
    east_sketch[1 : rows + 1, :, 0:lons] = dot(spread_signs[...], east_b[...]).reshape(rows, RANK, lons)
    for side, j in ((0, 1), (1, rows)):
        halo_send[side] = east_sketch[j].astype(BF16)
    pl.semaphore_wait(barrier, len(peers))
    halos = [
        remote(halo_send.at[0], halo_recv.at[1], halo_ssem.at[0], halo_rsem.at[1], north),
        remote(halo_send.at[1], halo_recv.at[0], halo_ssem.at[1], halo_rsem.at[0], south),
    ]
    for copy in halos:
        copy.start()
    loads[1].wait()
    north_sketch[:, :, 0:lons] = dot(spread_signs[...], north_b[...]).reshape(rows, RANK, lons)

    def roll_pair(tiles, lane):
        left = [pltpu.roll(t, LANE - 1, 1) for t in tiles]
        right = [pltpu.roll(t, 1, 1) for t in tiles]
        first_to_end = pltpu.roll(tiles[0], tail - 1, 1)
        end_to_first = pltpu.roll(tiles[-1], LANE - tail + 1, 1)
        result = []
        for c in range(n_col):
            if c < n_col - 1:
                nxt = jnp.where(lane < LANE - 1, left[c], left[c + 1])
            else:
                nxt = jnp.where(lane < tail - 1, left[c], first_to_end)
            prv = jnp.where(lane > 0, right[c], right[c - 1] if c > 0 else end_to_first)
            result.append(nxt - prv)
        return result

    def constants(j, count):
        def spread(t, i):
            return jnp.broadcast_to(t[i : i + 1, :], (count, LANE))

        return spread(cosines, j), spread(cosines, j + 2), spread(weights, j + 1)

    lane32 = iota((RANK, LANE), 1)

    def sketch_row(j):
        c_above, c_below, weight = constants(j, RANK)
        zonal = roll_pair([north_sketch[j, :, c * LANE : (c + 1) * LANE] for c in range(n_col)], lane32)
        for c in range(n_col):
            part = slice(c * LANE, (c + 1) * LANE)
            value = (zonal[c] - east_sketch[j, :, part] * c_above + east_sketch[j + 2, :, part] * c_below) * weight
            if c == n_col - 1:
                value = jnp.where(lane32 < tail, value, 0.0)
            sketch[j, :, part] = value

    lane16 = iota((16, LANE), 1)

    def field_row(j, east_above, east_below):
        c_above, c_below, weight = constants(j, 16)

        def group(g, carry):
            part = pl.ds(g * (16 * rows) + j, 16, stride=rows)
            zonal = roll_pair([north_f[c, part, :] for c in range(n_col)], lane16)
            for c in range(n_col):
                value = (zonal[c] - east_above(g, c) * c_above + east_below(g, c) * c_below) * weight
                if c == n_col - 1:
                    value = jnp.where(lane16 < tail, value, 0.0)
                field[j, pl.ds(g * 16, 16), c * LANE : (c + 1) * LANE] = value.astype(BF16)
            return carry

        lax.fori_loop(0, padded // 16, group, 0)

    def local_east(j):
        return lambda g, c: east_f[c, pl.ds(g * (16 * rows) + j, 16, stride=rows), :]

    def halo_east(side):
        return lambda g, c: edge_recv[side, pl.ds(g * 16, 16), c * LANE : (c + 1) * LANE].astype(F32)

    def widen(flat, wide):
        def run():
            for c in range(n_col):
                w = LANE if c < n_col - 1 else tail
                wide[c, 0:depth, 0:w] = flat[:, c * LANE : c * LANE + w].astype(F32)

        return run

    def send_edges():
        for side, j in ((0, 0), (1, rows - 1)):
            for c in range(n_col):
                edge_send[side, :, c * LANE : (c + 1) * LANE] = east_f[
                    c, pl.ds(j, padded, stride=rows), :
                ].astype(BF16)
        for copy in edges:
            copy.start()

    edges = [
        remote(edge_send.at[0], edge_recv.at[1], edge_ssem.at[0], edge_rsem.at[1], north),
        remote(edge_send.at[1], edge_recv.at[0], edge_ssem.at[1], edge_rsem.at[0], south),
    ]

    def field_task(j):
        if 0 < j < rows - 1:
            return lambda: field_row(j, local_east(j - 1), local_east(j + 1))
        if j == 0:
            def run():
                edges[1].wait_recv()
                field_row(0, halo_east(0), local_east(1))
        else:
            def run():
                edges[0].wait_recv()
                field_row(j, local_east(j - 1), halo_east(1))
        return run

    tasks = [widen(east_b, east_f), send_edges, widen(north_b, north_f)]
    tasks += [field_task(j) for j in list(range(1, rows - 1)) + [0, rows - 1]]

    def work(count):
        for _ in range(min(count, len(tasks))):
            tasks.pop(0)()

    far, mid, near, summed = range(4)
    reach = (4, 3, 1, 2)
    route = (2, 1, 1, 2)
    toward = (-1, 1)
    halves = (list(range(0, NSUB // 2)), list(range(NSUB // 2, NSUB)))
    order = [h for pair in zip(halves[0], halves[1]) for h in pair]
    pieces = ([h for pair in zip(halves[1], halves[0]) for h in pair], order)

    def cols(h):
        return pl.ds(h * piece, piece)

    def row_at(offset):
        return lax.rem(m + n_tm + offset, n_tm)

    def chain(side, kind, h):
        return remote(
            chain_send.at[side, kind, :, cols(h)],
            chain_recv.at[side, kind, :, cols(h)],
            chain_ssem.at[side, kind, h],
            chain_rsem.at[side, kind, h],
            z_at(toward[side] * route[kind]),
        )

    def send_own(side, kind, h):
        j = row_at(toward[side] * reach[kind])
        chain_send[side, kind, :, cols(h)] = sketch[j, :, cols(h)].astype(BF16)
        chain(side, kind, h).start()

    def when_class(edge, offset, run):
        j = row_at(offset)
        is_edge = jnp.logical_or(j == 0, j == rows - 1)
        pl.when(is_edge if edge else jnp.logical_not(is_edge))(run)

    def begin(edge):
        for step in range(NSUB // 2):
            first = [pieces[side][2 * step] for side in (0, 1)]
            second = [pieces[side][2 * step + 1] for side in (0, 1)]
            for side in (0, 1):
                when_class(edge, toward[side] * reach[mid], lambda side=side: send_own(side, mid, first[side]))

            def send_far():
                for side in (0, 1):
                    send_own(side, far, second[side])

            when_class(edge, reach[far], send_far)
            for side in (0, 1):
                when_class(edge, toward[side] * reach[mid], lambda side=side: send_own(side, mid, second[side]))

    def begin_near(edge):
        for side in (0, 1):

            def run(side=side):
                for h in order:
                    send_own(side, near, h)

            when_class(edge, toward[side] * reach[near], run)

    def relay(edge):
        for i in range(NSUB):
            for side in (0, 1):

                def run(h=pieces[side][i], side=side):
                    j = row_at(toward[side] * 2)
                    value = sketch[j, :, cols(h)]
                    for kind in (mid, far) if h in halves[side] else (mid,):
                        chain(side, kind, h).wait_recv()
                        value = value + chain_recv[side, kind, :, cols(h)].astype(F32)
                    chain_send[side, summed, :, cols(h)] = value.astype(BF16)
                    chain(side, summed, h).start()

                when_class(edge, toward[side] * 2, run)

    to_one, to_two, to_three, to_four = range(4)
    stride_of = (1, 2, 1, 2)

    def gather(side, kind, h, j):
        return remote(
            whole.at[j, :, cols(h)],
            whole.at[j, :, cols(h)],
            gather_ssem.at[side, kind, h],
            gather_rsem.at[side, kind, h],
            z_at(toward[side] * stride_of[kind]),
        )

    def arrive(kind, edge):
        for h in order:
            for side in (0, 1):
                if kind == to_four and h not in halves[side]:
                    continue

                def run(h=h, side=side):
                    j = row_at(-toward[side] * (kind + 1))
                    gather(side, kind, h, j).wait_recv()
                    if kind == to_two:
                        if h in halves[side]:
                            gather(side, to_four, h, j).start()
                        gather(side, to_three, h, j).start()

                when_class(edge, -toward[side] * (kind + 1), run)

    def consume(j):
        projection[...] += dot_t(whole[j], field[j])

    class LatSum:
        def __init__(self, n):
            self.levels = (
                (x_slots.at[n], x_ssem.at[n], x_rsem.at[n], x * 2 + core, x_line, x_peer),
                (y_slots.at[n], y_ssem.at[n], y_rsem.at[n], y, y_line, y_peer),
            )

        def copy(self, level, i, slot):
            slots_of, ssem, rsem, _, line, _ = self.levels[level]
            return remote(slots_of.at[slot], slots_of.at[slot], ssem.at[i], rsem.at[i], line[i])

        def send(self, level, value):
            slots_of, _, _, here, line, _ = self.levels[level]
            slots_of[here] = value
            for i in range(len(line)):
                self.copy(level, i, here).start()

        def total(self, level):
            slots_of, _, _, _, line, peer_of = self.levels[level]
            for i in range(len(line)):
                self.copy(level, i, peer_of(i + 1, -1)).wait_recv()
            value = slots_of[0]
            for i in range(1, len(line) + 1):
                value = value + slots_of[i]
            return value

        def drain(self):
            for level, (_, _, _, here, line, _) in enumerate(self.levels):
                for i in range(len(line)):
                    self.copy(level, i, here).wait_send()

    def gram_copy(d, slot):
        return remote(
            gram_slots.at[slot], gram_slots.at[slot], gram_ssem.at[d - 1], gram_rsem.at[d - 1],
            {"tm": lax.rem(m + d, n_tm)},
        )

    gram_sum, projection_sum = LatSum(0), LatSum(1)
    projection[...] = jnp.zeros(projection.shape, F32)

    for j in range(1, rows - 1):
        sketch_row(j)
    begin(False)
    work(3)
    for side in (0, 1):
        halos[1 - side].wait_recv()
        east_sketch[side * (rows + 1)] = halo_recv[side].astype(F32)
    for j in (0, rows - 1):
        sketch_row(j)
    begin(True)
    begin_near(False)
    work(1)
    relay(False)
    begin_near(True)
    work(1)
    relay(True)
    work(2)
    for h in order:
        value = sketch[m, :, cols(h)]
        for kind in (near, summed):
            for side in (0, 1):
                chain(side, kind, h).wait_recv()
                value = value + chain_recv[side, kind, :, cols(h)].astype(F32)
        whole[m, :, cols(h)] = value.astype(BF16)
        for side in (0, 1):
            gather(side, to_two, h, m).start()
    for h in order:
        for side in (0, 1):
            gather(side, to_one, h, m).start()
    own = whole[m]
    gram_part[...] = jnp.zeros((RANK, LANE), F32)
    gram_part[:, 0:RANK] = dot_t(own, own)
    gram_sum.send(0, gram_part[...])
    work(2)
    gram_sum.send(1, gram_sum.total(0))
    arrive(to_two, False)
    work(1)
    arrive(to_two, True)
    work(len(tasks))
    for offset in (0, -2, 2):
        consume(row_at(offset))
    gram_slots[m] = gram_sum.total(1)
    for d in range(1, n_tm):
        gram_copy(d, m).start()
    for kind, offset in ((to_one, 1), (to_three, 3)):
        for edge in (False, True):
            arrive(kind, edge)
        for side in (0, 1):
            consume(row_at(-toward[side] * offset))
    for edge in (False, True):
        arrive(to_four, edge)
    consume(row_at(4))
    projection_sum.send(0, projection[...])
    for d in range(1, n_tm):
        gram_copy(d, lax.rem(m + n_tm - d, n_tm)).wait_recv()
    gram = gram_slots[0]
    for i in range(1, n_tm):
        gram = gram + gram_slots[i]
    inverse = inverse_factor(gram * (1.0 / cells))
    projection_sum.send(1, projection_sum.total(0))

    size = RANK * rows
    take_row = (iota((size, RANK), 0) // rows == iota((size, RANK), 1)).astype(F32).astype(BF16)
    take_col = (iota((RANK, size), 0) == lax.rem(iota((RANK, size), 1), RANK)).astype(F32).astype(BF16)
    same = lax.rem(iota((size, size), 0), rows) == iota((size, size), 1) // RANK
    flat = whole[...].reshape(size, width)
    basis = None
    for half in split(inverse):
        spread = dot(take_row, half).astype(BF16)
        spread = dot(spread, take_col)
        spread = jnp.where(same, spread, 0.0).astype(BF16)
        term = dot(spread, flat)
        basis = term if basis is None else basis + term
    basis_ref[...] = basis.reshape(RANK, rows, width)[:, :, :lons].astype(BF16)
    projected = projection_sum.total(1)
    coeffs = dot(inverse, projected, HIGHEST) * (1.0 / cells)
    coeffs = jnp.where(iota((RANK, padded), 1) < count_ref[0], coeffs, 0.0)
    coeffs_ref[...] = coeffs[:, :slots]

    for copy in halos + edges:
        copy.wait_send()
    for side in (0, 1):
        for kind in range(4):
            for h in range(NSUB):
                if kind != far or h in halves[side]:
                    chain(side, kind, h).wait_send()
                if kind != to_four or h in halves[side]:
                    gather(side, kind, h, m).wait_send()
    for part in (gram_sum, projection_sum):
        part.drain()
    for d in range(1, n_tm):
        gram_copy(d, m).wait_send()


def write_kernel(basis_ref, coeffs_ref, basis_out, coeffs_out):
    basis_out[...] = basis_ref[...]
    coeffs_out[...] = coeffs_ref[...]


def local(n_tm, n_lat, n_x, wind_east, wind_north, snap_counts, snap_ids):
    slots, rows, lons = wind_east.shape
    padded = -(-slots // LANE) * LANE
    n_col = -(-lons // LANE)
    width = n_col * LANE
    n_y = n_lat // (2 * n_x)
    ids = snap_ids.reshape(1, slots)
    shape = (slots, rows, lons, n_tm, n_lat, n_x)
    dma = pltpu.SemaphoreType.DMA
    in_vmem = pl.BlockSpec(memory_space=pltpu.VMEM)
    results = (jax.ShapeDtypeStruct((RANK, rows, lons), BF16), jax.ShapeDtypeStruct((RANK, slots), F32))
    found = pl.pallas_call(
        functools.partial(kernel, shape),
        out_shape=results,
        in_specs=[
            pl.BlockSpec(memory_space=pl.ANY),
            pl.BlockSpec(memory_space=pl.ANY),
            pl.BlockSpec(memory_space=pltpu.SMEM),
            pl.BlockSpec(memory_space=pltpu.VMEM),
        ],
        out_specs=(pl.BlockSpec(memory_space=pltpu.VMEM), pl.BlockSpec(memory_space=pltpu.VMEM)),
        scratch_shapes=[
            pltpu.VMEM((n_col, padded * rows, LANE), F32),
            pltpu.VMEM((n_col, padded * rows, LANE), F32),
            pltpu.VMEM((slots * rows, lons), BF16),
            pltpu.VMEM((slots * rows, lons), BF16),
            pltpu.VMEM((rows * RANK, slots * rows), BF16),
            pltpu.VMEM((rows + 2, RANK, width), F32),
            pltpu.VMEM((rows, RANK, width), F32),
            pltpu.VMEM((rows, RANK, width), F32),
            pltpu.VMEM((2, RANK, width), BF16),
            pltpu.VMEM((2, RANK, width), BF16),
            pltpu.VMEM((2, padded, width), BF16),
            pltpu.VMEM((2, padded, width), BF16),
            pltpu.VMEM((rows, padded, width), BF16),
            pltpu.VMEM((2, 4, RANK, width), BF16),
            pltpu.VMEM((2, 4, RANK, width), BF16),
            pltpu.VMEM((rows, RANK, width), BF16),
            pltpu.VMEM((RANK, padded), F32),
            pltpu.VMEM((RANK, LANE), F32),
            pltpu.VMEM((n_tm, RANK, LANE), F32),
            pltpu.VMEM((2, 2 * n_x, RANK, LANE), F32),
            pltpu.VMEM((2, n_y, RANK, LANE), F32),
            dma((2,)),
            dma((2,)),
            dma((2,)),
            dma((2,)),
            dma((2,)),
            dma((2, 4, NSUB)),
            dma((2, 4, NSUB)),
            dma((2, 4, NSUB)),
            dma((2, 4, NSUB)),
            dma((n_tm - 1,)),
            dma((n_tm - 1,)),
            dma((2, 2 * n_x - 1)),
            dma((2, 2 * n_x - 1)),
            dma((2, n_y - 1)),
            dma((2, n_y - 1)),
        ],
        compiler_params=pltpu.CompilerParams(
            collective_id=0, has_side_effects=True, vmem_limit_bytes=60 * 1024 * 1024
        ),
        name="eof",
    )(
        wind_east.reshape(slots * rows, lons), wind_north.reshape(slots * rows, lons), snap_counts, ids
    )
    return pl.pallas_call(
        write_kernel, out_shape=results, in_specs=[in_vmem, in_vmem], out_specs=(in_vmem, in_vmem), name="write"
    )(*found)


def solution(mesh):
    in_specs = (P("tm", "lat", None), P("tm", "lat", None), P("tm"), P("tm"))
    out_specs = (P(None, "lat", None), P(None, "tm"))
    body = functools.partial(local, mesh.shape["tm"], mesh.shape["lat"], 4)
    return jax.shard_map(body, mesh=mesh, in_specs=in_specs, out_specs=out_specs, check_vma=False)
```

```python
import functools

import jax
import jax.numpy as jnp
import numpy as np
from jax import lax
from jax.experimental import pallas as pl
from jax.experimental.pallas import tpu as pltpu
from jax.sharding import PartitionSpec as P

RANK = 32
LANE = 128
F32 = jnp.float32
BF16 = jnp.bfloat16
MESH = pl.DeviceIdType.MESH
HIGHEST = lax.Precision.HIGHEST
NSUB = 4


def dot(a, b, precision=None):
    return lax.dot_general(
        a, b, (((1,), (0,)), ((), ())), precision=precision, preferred_element_type=F32
    )


def dot_t(a, b, precision=None):
    return lax.dot_general(
        a, b, (((1,), (1,)), ((), ())), precision=precision, preferred_element_type=F32
    )


def iota(shape, dim):
    return lax.broadcasted_iota(jnp.int32, shape, dim)


def split(x):
    high = x.astype(BF16)
    return high, (x - high.astype(F32)).astype(BF16)


def cosine(x):
    y = x * x
    p = jnp.full_like(y, -1.0 / 3628800.0)
    for coefficient in (1.0 / 40320.0, -1.0 / 720.0, 1.0 / 24.0, -0.5, 1.0):
        p = p * y + coefficient
    return p


def inverse_factor(gram):
    row, lane = iota((RANK, LANE), 0), iota((RANK, LANE), 1)
    a = jnp.where(lane == row + RANK, 1.0, gram)
    for k in range(RANK - 1):
        pivot_row = a[k : k + 1, :]
        column = a[:, k : k + 1]
        factor = column / a[k : k + 1, k : k + 1]
        a = a - jnp.where(row > k, factor * pivot_row, 0.0)
    diagonal = jnp.sum(jnp.where(row == lane, a, 0.0), axis=1, keepdims=True)
    scaled = a * lax.rsqrt(diagonal)
    return pltpu.roll(scaled, LANE - RANK, 1)[:, :RANK]


def kernel(
    shape,
    east_hbm,
    north_hbm,
    count_hbm,
    ids_ref,
    basis_ref,
    coeffs_ref,
    east_f,
    north_f,
    east_b,
    north_b,
    spread_signs,
    east_sketch,
    north_sketch,
    sketch,
    halo_send,
    halo_recv,
    edge_send,
    edge_recv,
    field,
    chain_send,
    chain_recv,
    whole,
    projection,
    gram_part,
    gram_slots,
    x_slots,
    y_slots,
    count_ref,
    load_sem,
    halo_ssem,
    halo_rsem,
    edge_ssem,
    edge_rsem,
    chain_ssem,
    chain_rsem,
    gather_ssem,
    gather_rsem,
    gram_ssem,
    gram_rsem,
    x_ssem,
    x_rsem,
    y_ssem,
    y_rsem,
):
    slots, rows, lons, n_tm, n_lat, n_x = shape
    n_y = n_lat // (2 * n_x)
    n_col = pl.cdiv(lons, LANE)
    tail = lons - (n_col - 1) * LANE
    padded = field.shape[1]
    width = n_col * LANE
    piece = width // NSUB
    total_rows = rows * n_lat
    cells = total_rows * lons

    m = lax.axis_index("tm")
    b = lax.axis_index("lat")
    core = lax.rem(b, 2)
    x = lax.rem(b // 2, n_x)
    y = b // (2 * n_x)
    south, north = {"lat": lax.rem(b + 1, n_lat)}, {"lat": lax.rem(b + n_lat - 1, n_lat)}

    def z_at(d):
        return {"tm": lax.rem(m + n_tm + d, n_tm)}

    def x_peer(i, sign=1):
        dx, flip = i // 2, i % 2
        other = core + flip - 2 * flip * core
        return lax.rem(x + n_x + sign * dx, n_x) * 2 + other

    def y_peer(d, sign=1):
        return lax.rem(y + n_y + sign * d, n_y)

    x_line = [{"lat": y * (2 * n_x) + x_peer(i)} for i in range(1, 2 * n_x)]
    y_line = [{"lat": y_peer(d) * (2 * n_x) + x * 2 + core} for d in range(1, n_y)]
    peers = [z_at(d) for d in (-2, -1, 1, 2)] + [south, north] + x_line + y_line
    barrier = pltpu.get_barrier_semaphore()
    for peer in peers:
        pl.semaphore_signal(barrier, inc=1, device_id=peer, device_id_type=MESH)

    def remote(src, dst, ssem, rsem, peer):
        return pltpu.make_async_remote_copy(
            src_ref=src, dst_ref=dst, send_sem=ssem, recv_sem=rsem, device_id=peer, device_id_type=MESH
        )

    middle = slots * rows // 2
    ends = [slice(0, middle), slice(middle, slots * rows)]
    loads = [pltpu.make_async_copy(count_hbm, count_ref, load_sem.at[3])]
    loads += [pltpu.make_async_copy(east_hbm.at[part], east_b.at[part], load_sem.at[i]) for i, part in enumerate(ends)]
    loads += [pltpu.make_async_copy(north_hbm, north_b, load_sem.at[2])]
    for copy in loads:
        copy.start()
    loads[0].wait()

    ids = jnp.broadcast_to(ids_ref[...], (RANK, slots))
    column = iota((RANK, slots), 0)
    mixed = ids * 1103515245 + column * 40503 + 12345
    mixed = jnp.bitwise_xor(mixed, jnp.right_shift(mixed, 13))
    mixed = mixed * 1664525 + 1013904223
    mixed = jnp.bitwise_xor(mixed, jnp.right_shift(mixed, 16))
    flipped = jnp.bitwise_and(jnp.right_shift(mixed, 7), 1)
    slot_used = iota((RANK, slots), 1) < count_ref[0]
    signs = jnp.where(slot_used, (1 - 2 * flipped).astype(F32), 0.0).astype(BF16)
    depth = slots * rows
    repeat = (iota((slots, depth), 1) // rows == iota((slots, depth), 0)).astype(F32).astype(BF16)
    repeated = dot(signs, repeat)
    lane_row = lax.rem(iota((RANK, depth), 1), rows)
    for j in range(rows):
        spread_signs[j * RANK : (j + 1) * RANK, :] = jnp.where(lane_row == j, repeated, 0.0).astype(BF16)

    band_row = iota((16, LANE), 0) + (b * rows - 1)
    cosines = cosine((total_rows // 2 - band_row).astype(F32) * (jnp.pi / 720.0))
    weights = 0.5 / jnp.sqrt(cosines)
    inside = jnp.logical_and(band_row >= 0, band_row < total_rows)
    cosines = jnp.where(inside, cosines, 0.0)

    for wide in (east_f, north_f):
        wide[:, depth:, :] = jnp.zeros((n_col, padded * rows - depth, LANE), F32)

    for i, part in enumerate(ends):
        loads[1 + i].wait()
        partial = dot(spread_signs[:, part], east_b[part, :]).reshape(rows, RANK, lons)
        if i > 0:
            partial = east_sketch[1 : rows + 1, :, 0:lons] + partial
        east_sketch[1 : rows + 1, :, 0:lons] = partial
    for side, j in ((0, 1), (1, rows)):
        halo_send[side] = east_sketch[j].astype(BF16)
    pl.semaphore_wait(barrier, len(peers))
    halos = [
        remote(halo_send.at[0], halo_recv.at[1], halo_ssem.at[0], halo_rsem.at[1], north),
        remote(halo_send.at[1], halo_recv.at[0], halo_ssem.at[1], halo_rsem.at[0], south),
    ]
    for copy in halos:
        copy.start()
    loads[3].wait()
    north_sketch[:, :, 0:lons] = dot(spread_signs[...], north_b[...]).reshape(rows, RANK, lons)

    def roll_pair(tiles, lane):
        left = [pltpu.roll(t, LANE - 1, 1) for t in tiles]
        right = [pltpu.roll(t, 1, 1) for t in tiles]
        first_to_end = pltpu.roll(tiles[0], tail - 1, 1)
        end_to_first = pltpu.roll(tiles[-1], LANE - tail + 1, 1)
        result = []
        for c in range(n_col):
            if c < n_col - 1:
                nxt = jnp.where(lane < LANE - 1, left[c], left[c + 1])
            else:
                nxt = jnp.where(lane < tail - 1, left[c], first_to_end)
            prv = jnp.where(lane > 0, right[c], right[c - 1] if c > 0 else end_to_first)
            result.append(nxt - prv)
        return result

    def constants(j, count):
        def spread(t, i):
            return jnp.broadcast_to(t[i : i + 1, :], (count, LANE))

        return spread(cosines, j), spread(cosines, j + 2), spread(weights, j + 1)

    lane32 = iota((RANK, LANE), 1)

    def sketch_row(j):
        c_above, c_below, weight = constants(j, RANK)
        zonal = roll_pair([north_sketch[j, :, c * LANE : (c + 1) * LANE] for c in range(n_col)], lane32)
        for c in range(n_col):
            part = slice(c * LANE, (c + 1) * LANE)
            value = (zonal[c] - east_sketch[j, :, part] * c_above + east_sketch[j + 2, :, part] * c_below) * weight
            if c == n_col - 1:
                value = jnp.where(lane32 < tail, value, 0.0)
            sketch[j, :, part] = value

    lane16 = iota((16, LANE), 1)

    def field_row(j, east_above, east_below):
        c_above, c_below, weight = constants(j, 16)

        def group(g, carry):
            part = pl.ds(g * (16 * rows) + j, 16, stride=rows)
            zonal = roll_pair([north_f[c, part, :] for c in range(n_col)], lane16)
            for c in range(n_col):
                value = (zonal[c] - east_above(g, c) * c_above + east_below(g, c) * c_below) * weight
                if c == n_col - 1:
                    value = jnp.where(lane16 < tail, value, 0.0)
                field[j, pl.ds(g * 16, 16), c * LANE : (c + 1) * LANE] = value.astype(BF16)
            return carry

        lax.fori_loop(0, padded // 16, group, 0)

    def local_east(j):
        return lambda g, c: east_f[c, pl.ds(g * (16 * rows) + j, 16, stride=rows), :]

    def halo_east(side):
        return lambda g, c: edge_recv[side, pl.ds(g * 16, 16), c * LANE : (c + 1) * LANE].astype(F32)

    def widen(flat, wide):
        def run():
            for c in range(n_col):
                w = LANE if c < n_col - 1 else tail
                wide[c, 0:depth, 0:w] = flat[:, c * LANE : c * LANE + w].astype(F32)

        return run

    def send_edges():
        for side, j in ((0, 0), (1, rows - 1)):
            for c in range(n_col):
                edge_send[side, :, c * LANE : (c + 1) * LANE] = east_f[
                    c, pl.ds(j, padded, stride=rows), :
                ].astype(BF16)
        for copy in edges:
            copy.start()

    edges = [
        remote(edge_send.at[0], edge_recv.at[1], edge_ssem.at[0], edge_rsem.at[1], north),
        remote(edge_send.at[1], edge_recv.at[0], edge_ssem.at[1], edge_rsem.at[0], south),
    ]

    def field_task(j):
        if 0 < j < rows - 1:
            return lambda: field_row(j, local_east(j - 1), local_east(j + 1))
        if j == 0:
            def run():
                edges[1].wait_recv()
                field_row(0, halo_east(0), local_east(1))
        else:
            def run():
                edges[0].wait_recv()
                field_row(j, local_east(j - 1), halo_east(1))
        return run

    tasks = [widen(east_b, east_f), send_edges, widen(north_b, north_f)]
    tasks += [field_task(j) for j in list(range(1, rows - 1)) + [0, rows - 1]]

    def work(count):
        for _ in range(min(count, len(tasks))):
            tasks.pop(0)()

    far, mid, near, summed = range(4)
    reach = (4, 3, 1, 2)
    route = (2, 1, 1, 2)
    toward = (-1, 1)
    halves = (list(range(0, NSUB // 2)), list(range(NSUB // 2, NSUB)))
    order = [h for pair in zip(halves[0], halves[1]) for h in pair]
    pieces = ([h for pair in zip(halves[1], halves[0]) for h in pair], order)

    def cols(h):
        return pl.ds(h * piece, piece)

    def row_at(offset):
        return lax.rem(m + n_tm + offset, n_tm)

    def chain(side, kind, h):
        return remote(
            chain_send.at[side, kind, :, cols(h)],
            chain_recv.at[side, kind, :, cols(h)],
            chain_ssem.at[side, kind, h],
            chain_rsem.at[side, kind, h],
            z_at(toward[side] * route[kind]),
        )

    def send_own(side, kind, h):
        j = row_at(toward[side] * reach[kind])
        chain_send[side, kind, :, cols(h)] = sketch[j, :, cols(h)].astype(BF16)
        chain(side, kind, h).start()

    def when_class(edge, offset, run):
        j = row_at(offset)
        is_edge = jnp.logical_or(j == 0, j == rows - 1)
        pl.when(is_edge if edge else jnp.logical_not(is_edge))(run)

    def begin(edge):
        for step in range(NSUB // 2):
            first = [pieces[side][2 * step] for side in (0, 1)]
            second = [pieces[side][2 * step + 1] for side in (0, 1)]
            for side in (0, 1):
                when_class(edge, toward[side] * reach[mid], lambda side=side: send_own(side, mid, first[side]))

            def send_far():
                for side in (0, 1):
                    send_own(side, far, second[side])

            when_class(edge, reach[far], send_far)
            for side in (0, 1):
                when_class(edge, toward[side] * reach[mid], lambda side=side: send_own(side, mid, second[side]))

    def begin_near(edge):
        for side in (0, 1):

            def run(side=side):
                for h in order:
                    send_own(side, near, h)

            when_class(edge, toward[side] * reach[near], run)

    def relay(edge):
        for i in range(NSUB):
            for side in (0, 1):

                def run(h=pieces[side][i], side=side):
                    j = row_at(toward[side] * 2)
                    value = sketch[j, :, cols(h)]
                    for kind in (mid, far) if h in halves[side] else (mid,):
                        chain(side, kind, h).wait_recv()
                        value = value + chain_recv[side, kind, :, cols(h)].astype(F32)
                    chain_send[side, summed, :, cols(h)] = value.astype(BF16)
                    chain(side, summed, h).start()

                when_class(edge, toward[side] * 2, run)

    to_one, to_two, to_three, to_four = range(4)
    stride_of = (1, 2, 1, 2)

    def gather(side, kind, h, j):
        return remote(
            whole.at[j, :, cols(h)],
            whole.at[j, :, cols(h)],
            gather_ssem.at[side, kind, h],
            gather_rsem.at[side, kind, h],
            z_at(toward[side] * stride_of[kind]),
        )

    def arrive(kind, edge):
        for h in order:
            for side in (0, 1):
                if kind == to_four and h not in halves[side]:
                    continue

                def run(h=h, side=side):
                    j = row_at(-toward[side] * (kind + 1))
                    gather(side, kind, h, j).wait_recv()
                    if kind == to_two:
                        if h in halves[side]:
                            gather(side, to_four, h, j).start()
                        gather(side, to_three, h, j).start()

                when_class(edge, -toward[side] * (kind + 1), run)

    def consume(j):
        projection[...] += dot_t(whole[j], field[j])

    class LatSum:
        def __init__(self, n):
            self.levels = (
                (x_slots.at[n], x_ssem.at[n], x_rsem.at[n], x * 2 + core, x_line, x_peer),
                (y_slots.at[n], y_ssem.at[n], y_rsem.at[n], y, y_line, y_peer),
            )

        def copy(self, level, i, slot):
            slots_of, ssem, rsem, _, line, _ = self.levels[level]
            return remote(slots_of.at[slot], slots_of.at[slot], ssem.at[i], rsem.at[i], line[i])

        def send(self, level, value):
            slots_of, _, _, here, line, _ = self.levels[level]
            slots_of[here] = value
            for i in range(len(line)):
                self.copy(level, i, here).start()

        def total(self, level):
            slots_of, _, _, _, line, peer_of = self.levels[level]
            for i in range(len(line)):
                self.copy(level, i, peer_of(i + 1, -1)).wait_recv()
            value = slots_of[0]
            for i in range(1, len(line) + 1):
                value = value + slots_of[i]
            return value

        def drain(self):
            for level, (_, _, _, here, line, _) in enumerate(self.levels):
                for i in range(len(line)):
                    self.copy(level, i, here).wait_send()

    def gram_copy(d, slot):
        return remote(
            gram_slots.at[slot], gram_slots.at[slot], gram_ssem.at[d - 1], gram_rsem.at[d - 1],
            {"tm": lax.rem(m + d, n_tm)},
        )

    gram_sum, projection_sum = LatSum(0), LatSum(1)
    projection[...] = jnp.zeros(projection.shape, F32)

    for j in range(1, rows - 1):
        sketch_row(j)
    begin(False)
    work(3)
    for side in (0, 1):
        halos[1 - side].wait_recv()
        east_sketch[side * (rows + 1)] = halo_recv[side].astype(F32)
    for j in (0, rows - 1):
        sketch_row(j)
    begin(True)
    begin_near(False)
    work(1)
    relay(False)
    begin_near(True)
    work(1)
    relay(True)
    work(2)
    for h in order:
        value = sketch[m, :, cols(h)]
        for kind in (near, summed):
            for side in (0, 1):
                chain(side, kind, h).wait_recv()
                value = value + chain_recv[side, kind, :, cols(h)].astype(F32)
        whole[m, :, cols(h)] = value.astype(BF16)
        for side in (0, 1):
            gather(side, to_two, h, m).start()
    for h in order:
        for side in (0, 1):
            gather(side, to_one, h, m).start()
    own = whole[m]
    gram_part[...] = jnp.zeros((RANK, LANE), F32)
    gram_part[:, 0:RANK] = dot_t(own, own)
    gram_sum.send(0, gram_part[...])
    work(2)
    arrive(to_two, False)
    gram_sum.send(1, gram_sum.total(0))
    work(1)
    arrive(to_two, True)
    work(len(tasks))
    for offset in (0, -2, 2):
        consume(row_at(offset))
    gram_slots[m] = gram_sum.total(1)
    for d in range(1, n_tm):
        gram_copy(d, m).start()
    for kind, offset in ((to_one, 1), (to_three, 3)):
        for edge in (False, True):
            arrive(kind, edge)
        for side in (0, 1):
            consume(row_at(-toward[side] * offset))
    for edge in (False, True):
        arrive(to_four, edge)
    consume(row_at(4))
    projection_sum.send(0, projection[...])
    for d in range(1, n_tm):
        gram_copy(d, lax.rem(m + n_tm - d, n_tm)).wait_recv()
    gram = gram_slots[0]
    for i in range(1, n_tm):
        gram = gram + gram_slots[i]
    inverse = inverse_factor(gram * (1.0 / cells))
    projection_sum.send(1, projection_sum.total(0))

    size = RANK * rows
    take_row = (iota((size, RANK), 0) // rows == iota((size, RANK), 1)).astype(F32).astype(BF16)
    take_col = (iota((RANK, size), 0) == lax.rem(iota((RANK, size), 1), RANK)).astype(F32).astype(BF16)
    same = lax.rem(iota((size, size), 0), rows) == iota((size, size), 1) // RANK
    flat = whole[...].reshape(size, width)
    basis = None
    for half in split(inverse):
        spread = dot(take_row, half).astype(BF16)
        spread = dot(spread, take_col)
        spread = jnp.where(same, spread, 0.0).astype(BF16)
        term = dot(spread, flat)
        basis = term if basis is None else basis + term
    basis_ref[...] = basis.reshape(RANK, rows, width)[:, :, :lons].astype(BF16)
    projected = projection_sum.total(1)
    coeffs = dot(inverse, projected, HIGHEST) * (1.0 / cells)
    coeffs = jnp.where(iota((RANK, padded), 1) < count_ref[0], coeffs, 0.0)
    coeffs_ref[...] = coeffs[:, :slots]

    for copy in halos + edges:
        copy.wait_send()
    for side in (0, 1):
        for kind in range(4):
            for h in range(NSUB):
                if kind != far or h in halves[side]:
                    chain(side, kind, h).wait_send()
                if kind != to_four or h in halves[side]:
                    gather(side, kind, h, m).wait_send()
    for part in (gram_sum, projection_sum):
        part.drain()
    for d in range(1, n_tm):
        gram_copy(d, m).wait_send()


def local(n_tm, n_lat, n_x, wind_east, wind_north, snap_counts, snap_ids):
    slots, rows, lons = wind_east.shape
    padded = -(-slots // LANE) * LANE
    n_col = -(-lons // LANE)
    width = n_col * LANE
    n_y = n_lat // (2 * n_x)
    ids = snap_ids.reshape(1, slots)
    shape = (slots, rows, lons, n_tm, n_lat, n_x)
    dma = pltpu.SemaphoreType.DMA
    return pl.pallas_call(
        functools.partial(kernel, shape),
        out_shape=(pltpu.VMEM((RANK, rows, lons), BF16), pltpu.VMEM((RANK, slots), F32)),
        in_specs=[
            pl.BlockSpec(memory_space=pl.ANY),
            pl.BlockSpec(memory_space=pl.ANY),
            pl.BlockSpec(memory_space=pltpu.HBM),
            pl.BlockSpec(memory_space=pltpu.VMEM),
        ],
        out_specs=(pl.BlockSpec(memory_space=pltpu.VMEM), pl.BlockSpec(memory_space=pltpu.VMEM)),
        scratch_shapes=[
            pltpu.VMEM((n_col, padded * rows, LANE), F32),
            pltpu.VMEM((n_col, padded * rows, LANE), F32),
            pltpu.VMEM((slots * rows, lons), BF16),
            pltpu.VMEM((slots * rows, lons), BF16),
            pltpu.VMEM((rows * RANK, slots * rows), BF16),
            pltpu.VMEM((rows + 2, RANK, width), F32),
            pltpu.VMEM((rows, RANK, width), F32),
            pltpu.VMEM((rows, RANK, width), F32),
            pltpu.VMEM((2, RANK, width), BF16),
            pltpu.VMEM((2, RANK, width), BF16),
            pltpu.VMEM((2, padded, width), BF16),
            pltpu.VMEM((2, padded, width), BF16),
            pltpu.VMEM((rows, padded, width), BF16),
            pltpu.VMEM((2, 4, RANK, width), BF16),
            pltpu.VMEM((2, 4, RANK, width), BF16),
            pltpu.VMEM((rows, RANK, width), BF16),
            pltpu.VMEM((RANK, padded), F32),
            pltpu.VMEM((RANK, LANE), F32),
            pltpu.VMEM((n_tm, RANK, LANE), F32),
            pltpu.VMEM((2, 2 * n_x, RANK, LANE), F32),
            pltpu.VMEM((2, n_y, RANK, LANE), F32),
            pltpu.SMEM((1,), jnp.int32),
            dma((4,)),
            dma((2,)),
            dma((2,)),
            dma((2,)),
            dma((2,)),
            dma((2, 4, NSUB)),
            dma((2, 4, NSUB)),
            dma((2, 4, NSUB)),
            dma((2, 4, NSUB)),
            dma((n_tm - 1,)),
            dma((n_tm - 1,)),
            dma((2, 2 * n_x - 1)),
            dma((2, 2 * n_x - 1)),
            dma((2, n_y - 1)),
            dma((2, n_y - 1)),
        ],
        compiler_params=pltpu.CompilerParams(
            collective_id=0, has_side_effects=True, vmem_limit_bytes=60 * 1024 * 1024
        ),
        name="eof",
    )(
        wind_east.reshape(slots * rows, lons), wind_north.reshape(slots * rows, lons), snap_counts, ids
    )


def solution(mesh):
    in_specs = (P("tm", "lat", None), P("tm", "lat", None), P("tm"), P("tm"))
    out_specs = (P(None, "lat", None), P(None, "tm"))
    body = functools.partial(local, mesh.shape["tm"], mesh.shape["lat"], 4)
    return jax.shard_map(body, mesh=mesh, in_specs=in_specs, out_specs=out_specs, check_vma=False)
```

```python
import functools

import jax
import jax.numpy as jnp
import numpy as np
from jax import lax
from jax.experimental import pallas as pl
from jax.experimental.pallas import tpu as pltpu
from jax.sharding import PartitionSpec as P

RANK = 32
LANE = 128
F32 = jnp.float32
BF16 = jnp.bfloat16
MESH = pl.DeviceIdType.MESH
HIGHEST = lax.Precision.HIGHEST
NSUB = 4


def dot(a, b, precision=None):
    return lax.dot_general(
        a, b, (((1,), (0,)), ((), ())), precision=precision, preferred_element_type=F32
    )


def dot_t(a, b, precision=None):
    return lax.dot_general(
        a, b, (((1,), (1,)), ((), ())), precision=precision, preferred_element_type=F32
    )


def iota(shape, dim):
    return lax.broadcasted_iota(jnp.int32, shape, dim)


def split(x):
    high = x.astype(BF16)
    return high, (x - high.astype(F32)).astype(BF16)


def cosine(x):
    y = x * x
    p = jnp.full_like(y, -1.0 / 3628800.0)
    for coefficient in (1.0 / 40320.0, -1.0 / 720.0, 1.0 / 24.0, -0.5, 1.0):
        p = p * y + coefficient
    return p


def inverse_factor(gram):
    row, lane = iota((RANK, LANE), 0), iota((RANK, LANE), 1)
    a = jnp.where(lane == row + RANK, 1.0, gram)
    for k in range(RANK - 1):
        pivot_row = a[k : k + 1, :]
        column = a[:, k : k + 1]
        factor = column / a[k : k + 1, k : k + 1]
        a = a - jnp.where(row > k, factor * pivot_row, 0.0)
    diagonal = jnp.sum(jnp.where(row == lane, a, 0.0), axis=1, keepdims=True)
    scaled = a * lax.rsqrt(diagonal)
    return pltpu.roll(scaled, LANE - RANK, 1)[:, :RANK]


def kernel(
    shape,
    east_hbm,
    north_hbm,
    count_hbm,
    ids_ref,
    basis_ref,
    coeffs_ref,
    east_f,
    north_f,
    east_b,
    north_b,
    spread_signs,
    east_sketch,
    north_sketch,
    sketch,
    halo_send,
    halo_recv,
    edge_send,
    edge_recv,
    field,
    chain_send,
    chain_recv,
    whole,
    projection,
    gram_part,
    gram_slots,
    gram_x,
    gram_y,
    projection_x,
    projection_y,
    count_ref,
    load_sem,
    halo_ssem,
    halo_rsem,
    edge_ssem,
    edge_rsem,
    chain_ssem,
    chain_rsem,
    gather_ssem,
    gather_rsem,
    gram_ssem,
    gram_rsem,
    x_ssem,
    x_rsem,
    y_ssem,
    y_rsem,
):
    slots, rows, lons, n_tm, n_lat, n_x = shape
    n_y = n_lat // (2 * n_x)
    n_col = pl.cdiv(lons, LANE)
    tail = lons - (n_col - 1) * LANE
    padded = field.shape[1]
    width = n_col * LANE
    piece = width // NSUB
    total_rows = rows * n_lat
    cells = total_rows * lons

    m = lax.axis_index("tm")
    b = lax.axis_index("lat")
    core = lax.rem(b, 2)
    x = lax.rem(b // 2, n_x)
    y = b // (2 * n_x)
    south, north = {"lat": lax.rem(b + 1, n_lat)}, {"lat": lax.rem(b + n_lat - 1, n_lat)}

    def z_at(d):
        return {"tm": lax.rem(m + n_tm + d, n_tm)}

    def x_peer(i, sign=1):
        dx, flip = i // 2, i % 2
        other = core + flip - 2 * flip * core
        return lax.rem(x + n_x + sign * dx, n_x) * 2 + other

    def y_peer(d, sign=1):
        return lax.rem(y + n_y + sign * d, n_y)

    x_line = [{"lat": y * (2 * n_x) + x_peer(i)} for i in range(1, 2 * n_x)]
    y_line = [{"lat": y_peer(d) * (2 * n_x) + x * 2 + core} for d in range(1, n_y)]
    peers = [z_at(d) for d in (-2, -1, 1, 2)] + [south, north] + x_line + y_line
    barrier = pltpu.get_barrier_semaphore()
    for peer in peers:
        pl.semaphore_signal(barrier, inc=1, device_id=peer, device_id_type=MESH)

    def remote(src, dst, ssem, rsem, peer):
        return pltpu.make_async_remote_copy(
            src_ref=src, dst_ref=dst, send_sem=ssem, recv_sem=rsem, device_id=peer, device_id_type=MESH
        )

    middle = slots * rows // 2
    ends = [slice(0, middle), slice(middle, slots * rows)]
    loads = [pltpu.make_async_copy(count_hbm, count_ref, load_sem.at[3])]
    loads += [pltpu.make_async_copy(east_hbm.at[part], east_b.at[part], load_sem.at[i]) for i, part in enumerate(ends)]
    loads += [pltpu.make_async_copy(north_hbm, north_b, load_sem.at[2])]
    for copy in loads:
        copy.start()
    loads[0].wait()

    ids = jnp.broadcast_to(ids_ref[...], (RANK, slots))
    column = iota((RANK, slots), 0)
    mixed = ids * 1103515245 + column * 40503 + 12345
    mixed = jnp.bitwise_xor(mixed, jnp.right_shift(mixed, 13))
    mixed = mixed * 1664525 + 1013904223
    mixed = jnp.bitwise_xor(mixed, jnp.right_shift(mixed, 16))
    flipped = jnp.bitwise_and(jnp.right_shift(mixed, 7), 1)
    slot_used = iota((RANK, slots), 1) < count_ref[0]
    signs = jnp.where(slot_used, (1 - 2 * flipped).astype(F32), 0.0).astype(BF16)
    depth = slots * rows
    repeat = (iota((slots, depth), 1) // rows == iota((slots, depth), 0)).astype(F32).astype(BF16)
    repeated = dot(signs, repeat)
    lane_row = lax.rem(iota((RANK, depth), 1), rows)
    for j in range(rows):
        spread_signs[j * RANK : (j + 1) * RANK, :] = jnp.where(lane_row == j, repeated, 0.0).astype(BF16)

    band_row = iota((16, LANE), 0) + (b * rows - 1)
    cosines = cosine((total_rows // 2 - band_row).astype(F32) * (jnp.pi / 720.0))
    weights = 0.5 / jnp.sqrt(cosines)
    inside = jnp.logical_and(band_row >= 0, band_row < total_rows)
    cosines = jnp.where(inside, cosines, 0.0)

    for wide in (east_f, north_f):
        wide[:, depth:, :] = jnp.zeros((n_col, padded * rows - depth, LANE), F32)

    for i, part in enumerate(ends):
        loads[1 + i].wait()
        partial = dot(spread_signs[:, part], east_b[part, :]).reshape(rows, RANK, lons)
        if i > 0:
            partial = east_sketch[1 : rows + 1, :, 0:lons] + partial
        east_sketch[1 : rows + 1, :, 0:lons] = partial
    for side, j in ((0, 1), (1, rows)):
        halo_send[side] = east_sketch[j].astype(BF16)
    pl.semaphore_wait(barrier, len(peers))

    def cols(h):
        return pl.ds(h * piece, piece)

    halves = (list(range(0, NSUB // 2)), list(range(NSUB // 2, NSUB)))
    order = [h for pair in zip(halves[0], halves[1]) for h in pair]

    def halo(side, h):
        return remote(
            halo_send.at[side, :, cols(h)],
            halo_recv.at[1 - side, :, cols(h)],
            halo_ssem.at[side, h],
            halo_rsem.at[1 - side, h],
            (north, south)[side],
        )

    for h in order:
        for side in (0, 1):
            halo(side, h).start()
    loads[3].wait()
    north_sketch[:, :, 0:lons] = dot(spread_signs[...], north_b[...]).reshape(rows, RANK, lons)

    def roll_pair(tiles, lane):
        left = [pltpu.roll(t, LANE - 1, 1) for t in tiles]
        right = [pltpu.roll(t, 1, 1) for t in tiles]
        first_to_end = pltpu.roll(tiles[0], tail - 1, 1)
        end_to_first = pltpu.roll(tiles[-1], LANE - tail + 1, 1)
        result = []
        for c in range(n_col):
            if c < n_col - 1:
                nxt = jnp.where(lane < LANE - 1, left[c], left[c + 1])
            else:
                nxt = jnp.where(lane < tail - 1, left[c], first_to_end)
            prv = jnp.where(lane > 0, right[c], right[c - 1] if c > 0 else end_to_first)
            result.append(nxt - prv)
        return result

    def constants(j, count):
        def spread(t, i):
            return jnp.broadcast_to(t[i : i + 1, :], (count, LANE))

        return spread(cosines, j), spread(cosines, j + 2), spread(weights, j + 1)

    lane32 = iota((RANK, LANE), 1)

    def sketch_row(j):
        c_above, c_below, weight = constants(j, RANK)
        zonal = roll_pair([north_sketch[j, :, c * LANE : (c + 1) * LANE] for c in range(n_col)], lane32)
        for c in range(n_col):
            part = slice(c * LANE, (c + 1) * LANE)
            value = zonal[c]
            if j > 0:
                value = value - east_sketch[j, :, part] * c_above
            if j < rows - 1:
                value = value + east_sketch[j + 2, :, part] * c_below
            value = value * weight
            if c == n_col - 1:
                value = jnp.where(lane32 < tail, value, 0.0)
            sketch[j, :, part] = value

    def add_halo(side, h):
        halo(1 - side, h).wait_recv()
        j = (0, rows - 1)[side]
        c_above, c_below, weight = constants(j, RANK)
        scale = (-c_above * weight, c_below * weight)[side]
        for c in range(h * (piece // LANE), (h + 1) * (piece // LANE)):
            part = slice(c * LANE, (c + 1) * LANE)
            value = halo_recv[side, :, part].astype(F32) * scale
            if c == n_col - 1:
                value = jnp.where(lane32 < tail, value, 0.0)
            sketch[j, :, part] += value

    lane16 = iota((16, LANE), 1)

    def field_row(j, east_above, east_below):
        c_above, c_below, weight = constants(j, 16)

        def group(g, carry):
            part = pl.ds(g * (16 * rows) + j, 16, stride=rows)
            zonal = roll_pair([north_f[c, part, :] for c in range(n_col)], lane16)
            for c in range(n_col):
                value = (zonal[c] - east_above(g, c) * c_above + east_below(g, c) * c_below) * weight
                if c == n_col - 1:
                    value = jnp.where(lane16 < tail, value, 0.0)
                field[j, pl.ds(g * 16, 16), c * LANE : (c + 1) * LANE] = value.astype(BF16)
            return carry

        lax.fori_loop(0, padded // 16, group, 0)

    def local_east(j):
        return lambda g, c: east_f[c, pl.ds(g * (16 * rows) + j, 16, stride=rows), :]

    def halo_east(side):
        return lambda g, c: edge_recv[side, pl.ds(g * 16, 16), c * LANE : (c + 1) * LANE].astype(F32)

    def widen(flat, wide):
        def run():
            for c in range(n_col):
                w = LANE if c < n_col - 1 else tail
                wide[c, 0:depth, 0:w] = flat[:, c * LANE : c * LANE + w].astype(F32)

        return run

    def send_edges():
        for side, j in ((0, 0), (1, rows - 1)):
            for c in range(n_col):
                edge_send[side, :, c * LANE : (c + 1) * LANE] = east_f[
                    c, pl.ds(j, padded, stride=rows), :
                ].astype(BF16)
        for copy in edges:
            copy.start()

    edges = [
        remote(edge_send.at[0], edge_recv.at[1], edge_ssem.at[0], edge_rsem.at[1], north),
        remote(edge_send.at[1], edge_recv.at[0], edge_ssem.at[1], edge_rsem.at[0], south),
    ]

    def field_task(j):
        if 0 < j < rows - 1:
            return lambda: field_row(j, local_east(j - 1), local_east(j + 1))
        if j == 0:
            def run():
                edges[1].wait_recv()
                field_row(0, halo_east(0), local_east(1))
        else:
            def run():
                edges[0].wait_recv()
                field_row(j, local_east(j - 1), halo_east(1))
        return run

    tasks = [widen(east_b, east_f), send_edges, widen(north_b, north_f)]
    tasks += [field_task(j) for j in list(range(1, rows - 1)) + [0, rows - 1]]

    def work(count):
        for _ in range(min(count, len(tasks))):
            tasks.pop(0)()

    far, mid, near, summed = range(4)
    reach = (4, 3, 1, 2)
    route = (2, 1, 1, 2)
    toward = (-1, 1)
    pieces = ([h for pair in zip(halves[1], halves[0]) for h in pair], order)

    def row_at(offset):
        return lax.rem(m + n_tm + offset, n_tm)

    def chain(side, kind, h):
        return remote(
            chain_send.at[side, kind, :, cols(h)],
            chain_recv.at[side, kind, :, cols(h)],
            chain_ssem.at[side, kind, h],
            chain_rsem.at[side, kind, h],
            z_at(toward[side] * route[kind]),
        )

    def send_own(side, kind, h):
        j = row_at(toward[side] * reach[kind])
        chain_send[side, kind, :, cols(h)] = sketch[j, :, cols(h)].astype(BF16)
        chain(side, kind, h).start()

    def when_class(edge, offset, run):
        j = row_at(offset)
        is_edge = jnp.logical_or(j == 0, j == rows - 1)
        pl.when(is_edge if edge else jnp.logical_not(is_edge))(run)

    def begin(edge):
        for step in range(NSUB // 2):
            if edge:
                for h in order[2 * step : 2 * step + 2]:
                    for side in (0, 1):
                        add_halo(side, h)
            first = [pieces[side][2 * step] for side in (0, 1)]
            second = [pieces[side][2 * step + 1] for side in (0, 1)]
            for side in (0, 1):
                when_class(edge, toward[side] * reach[mid], lambda side=side: send_own(side, mid, first[side]))

            def send_far():
                for side in (0, 1):
                    send_own(side, far, second[side])

            when_class(edge, reach[far], send_far)
            for side in (0, 1):
                when_class(edge, toward[side] * reach[mid], lambda side=side: send_own(side, mid, second[side]))

    def begin_near(edge):
        for side in (0, 1):

            def run(side=side):
                for h in order:
                    send_own(side, near, h)

            when_class(edge, toward[side] * reach[near], run)

    def relay(edge):
        for i in range(NSUB):
            for side in (0, 1):

                def run(h=pieces[side][i], side=side):
                    j = row_at(toward[side] * 2)
                    value = sketch[j, :, cols(h)]
                    for kind in (mid, far) if h in halves[side] else (mid,):
                        chain(side, kind, h).wait_recv()
                        value = value + chain_recv[side, kind, :, cols(h)].astype(F32)
                    chain_send[side, summed, :, cols(h)] = value.astype(BF16)
                    chain(side, summed, h).start()

                when_class(edge, toward[side] * 2, run)

    to_one, to_two, to_three, to_four = range(4)
    stride_of = (1, 2, 1, 2)

    def gather(side, kind, h, j):
        return remote(
            whole.at[j, :, cols(h)],
            whole.at[j, :, cols(h)],
            gather_ssem.at[side, kind, h],
            gather_rsem.at[side, kind, h],
            z_at(toward[side] * stride_of[kind]),
        )

    def arrive(kind, edge):
        for h in order:
            for side in (0, 1):
                if kind == to_four and h not in halves[side]:
                    continue

                def run(h=h, side=side):
                    j = row_at(-toward[side] * (kind + 1))
                    gather(side, kind, h, j).wait_recv()
                    if kind == to_two:
                        if h in halves[side]:
                            gather(side, to_four, h, j).start()
                        gather(side, to_three, h, j).start()

                when_class(edge, -toward[side] * (kind + 1), run)

    def consume(j):
        projection[...] += dot_t(whole[j], field[j])

    class LatSum:
        def __init__(self, n, x_slots, y_slots):
            self.levels = (
                (x_slots, x_ssem.at[n], x_rsem.at[n], x * 2 + core, x_line, x_peer),
                (y_slots, y_ssem.at[n], y_rsem.at[n], y, y_line, y_peer),
            )

        def copy(self, level, i, slot):
            slots_of, ssem, rsem, _, line, _ = self.levels[level]
            return remote(slots_of.at[slot], slots_of.at[slot], ssem.at[i], rsem.at[i], line[i])

        def send(self, level, value):
            slots_of, _, _, here, line, _ = self.levels[level]
            slots_of[here] = value.astype(slots_of.dtype)
            for i in range(len(line)):
                self.copy(level, i, here).start()

        def total(self, level):
            slots_of, _, _, _, line, peer_of = self.levels[level]
            for i in range(len(line)):
                self.copy(level, i, peer_of(i + 1, -1)).wait_recv()
            value = slots_of[0].astype(F32)
            for i in range(1, len(line) + 1):
                value = value + slots_of[i].astype(F32)
            return value

        def drain(self):
            for level, (_, _, _, here, line, _) in enumerate(self.levels):
                for i in range(len(line)):
                    self.copy(level, i, here).wait_send()

    def gram_copy(d, slot):
        return remote(
            gram_slots.at[slot], gram_slots.at[slot], gram_ssem.at[d - 1], gram_rsem.at[d - 1],
            {"tm": lax.rem(m + d, n_tm)},
        )

    gram_sum, projection_sum = LatSum(0, gram_x, gram_y), LatSum(1, projection_x, projection_y)
    projection[...] = jnp.zeros(projection.shape, F32)

    for j in range(1, rows - 1):
        sketch_row(j)
    begin(False)
    for j in (0, rows - 1):
        sketch_row(j)
    work(3)
    begin(True)
    begin_near(False)
    work(1)
    relay(False)
    begin_near(True)
    work(1)
    relay(True)
    work(2)
    for h in order:
        value = sketch[m, :, cols(h)]
        for kind in (near, summed):
            for side in (0, 1):
                chain(side, kind, h).wait_recv()
                value = value + chain_recv[side, kind, :, cols(h)].astype(F32)
        whole[m, :, cols(h)] = value.astype(BF16)
        for side in (0, 1):
            gather(side, to_two, h, m).start()
    for h in order:
        for side in (0, 1):
            gather(side, to_one, h, m).start()
    own = whole[m]
    gram_part[...] = jnp.zeros((RANK, LANE), F32)
    gram_part[:, 0:RANK] = dot_t(own, own)
    gram_sum.send(0, gram_part[...])
    work(2)
    arrive(to_two, False)
    gram_sum.send(1, gram_sum.total(0))
    work(1)
    arrive(to_two, True)
    work(len(tasks))
    for offset in (0, -2, 2):
        consume(row_at(offset))
    gram_slots[m] = gram_sum.total(1)
    for d in range(1, n_tm):
        gram_copy(d, m).start()
    for kind, offset in ((to_one, 1), (to_three, 3)):
        for edge in (False, True):
            arrive(kind, edge)
        for side in (0, 1):
            consume(row_at(-toward[side] * offset))
    for edge in (False, True):
        arrive(to_four, edge)
    consume(row_at(4))
    projection_sum.send(0, projection[...])
    for d in range(1, n_tm):
        gram_copy(d, lax.rem(m + n_tm - d, n_tm)).wait_recv()
    gram = gram_slots[0]
    for i in range(1, n_tm):
        gram = gram + gram_slots[i]
    inverse = inverse_factor(gram * (1.0 / cells))
    projection_sum.send(1, projection_sum.total(0))

    size = RANK * rows
    take_row = (iota((size, RANK), 0) // rows == iota((size, RANK), 1)).astype(F32).astype(BF16)
    take_col = (iota((RANK, size), 0) == lax.rem(iota((RANK, size), 1), RANK)).astype(F32).astype(BF16)
    same = lax.rem(iota((size, size), 0), rows) == iota((size, size), 1) // RANK
    flat = whole[...].reshape(size, width)
    basis = None
    for half in split(inverse):
        spread = dot(take_row, half).astype(BF16)
        spread = dot(spread, take_col)
        spread = jnp.where(same, spread, 0.0).astype(BF16)
        term = dot(spread, flat)
        basis = term if basis is None else basis + term
    basis_ref[...] = basis.reshape(RANK, rows, width)[:, :, :lons].astype(BF16)
    projected = projection_sum.total(1)
    coeffs = dot(inverse, projected, HIGHEST) * (1.0 / cells)
    coeffs = jnp.where(iota((RANK, padded), 1) < count_ref[0], coeffs, 0.0)
    coeffs_ref[...] = coeffs[:, :slots]

    for copy in edges:
        copy.wait_send()
    for side in (0, 1):
        for h in range(NSUB):
            halo(side, h).wait_send()
    for side in (0, 1):
        for kind in range(4):
            for h in range(NSUB):
                if kind != far or h in halves[side]:
                    chain(side, kind, h).wait_send()
                if kind != to_four or h in halves[side]:
                    gather(side, kind, h, m).wait_send()
    for part in (gram_sum, projection_sum):
        part.drain()
    for d in range(1, n_tm):
        gram_copy(d, m).wait_send()


def local(n_tm, n_lat, n_x, wind_east, wind_north, snap_counts, snap_ids):
    slots, rows, lons = wind_east.shape
    padded = -(-slots // LANE) * LANE
    n_col = -(-lons // LANE)
    width = n_col * LANE
    n_y = n_lat // (2 * n_x)
    ids = snap_ids.reshape(1, slots)
    shape = (slots, rows, lons, n_tm, n_lat, n_x)
    dma = pltpu.SemaphoreType.DMA
    return pl.pallas_call(
        functools.partial(kernel, shape),
        out_shape=(pltpu.VMEM((RANK, rows, lons), BF16), pltpu.VMEM((RANK, slots), F32)),
        in_specs=[
            pl.BlockSpec(memory_space=pl.ANY),
            pl.BlockSpec(memory_space=pl.ANY),
            pl.BlockSpec(memory_space=pltpu.HBM),
            pl.BlockSpec(memory_space=pltpu.VMEM),
        ],
        out_specs=(pl.BlockSpec(memory_space=pltpu.VMEM), pl.BlockSpec(memory_space=pltpu.VMEM)),
        scratch_shapes=[
            pltpu.VMEM((n_col, padded * rows, LANE), F32),
            pltpu.VMEM((n_col, padded * rows, LANE), F32),
            pltpu.VMEM((slots * rows, lons), BF16),
            pltpu.VMEM((slots * rows, lons), BF16),
            pltpu.VMEM((rows * RANK, slots * rows), BF16),
            pltpu.VMEM((rows + 2, RANK, width), F32),
            pltpu.VMEM((rows, RANK, width), F32),
            pltpu.VMEM((rows, RANK, width), F32),
            pltpu.VMEM((2, RANK, width), BF16),
            pltpu.VMEM((2, RANK, width), BF16),
            pltpu.VMEM((2, padded, width), BF16),
            pltpu.VMEM((2, padded, width), BF16),
            pltpu.VMEM((rows, padded, width), BF16),
            pltpu.VMEM((2, 4, RANK, width), BF16),
            pltpu.VMEM((2, 4, RANK, width), BF16),
            pltpu.VMEM((rows, RANK, width), BF16),
            pltpu.VMEM((RANK, padded), F32),
            pltpu.VMEM((RANK, LANE), F32),
            pltpu.VMEM((n_tm, RANK, LANE), F32),
            pltpu.VMEM((2 * n_x, RANK, LANE), F32),
            pltpu.VMEM((n_y, RANK, LANE), F32),
            pltpu.VMEM((2 * n_x, RANK, padded), BF16),
            pltpu.VMEM((n_y, RANK, padded), BF16),
            pltpu.SMEM((1,), jnp.int32),
            dma((4,)),
            dma((2, NSUB)),
            dma((2, NSUB)),
            dma((2,)),
            dma((2,)),
            dma((2, 4, NSUB)),
            dma((2, 4, NSUB)),
            dma((2, 4, NSUB)),
            dma((2, 4, NSUB)),
            dma((n_tm - 1,)),
            dma((n_tm - 1,)),
            dma((2, 2 * n_x - 1)),
            dma((2, 2 * n_x - 1)),
            dma((2, n_y - 1)),
            dma((2, n_y - 1)),
        ],
        compiler_params=pltpu.CompilerParams(
            collective_id=0, has_side_effects=True, vmem_limit_bytes=60 * 1024 * 1024
        ),
        name="eof",
    )(
        wind_east.reshape(slots * rows, lons), wind_north.reshape(slots * rows, lons), snap_counts, ids
    )


def solution(mesh):
    in_specs = (P("tm", "lat", None), P("tm", "lat", None), P("tm"), P("tm"))
    out_specs = (P(None, "lat", None), P(None, "tm"))
    body = functools.partial(local, mesh.shape["tm"], mesh.shape["lat"], 4)
    return jax.shard_map(body, mesh=mesh, in_specs=in_specs, out_specs=out_specs, check_vma=False)
```

```python
import functools

import jax
import jax.numpy as jnp
import numpy as np
from jax import lax
from jax.experimental import pallas as pl
from jax.experimental.pallas import tpu as pltpu
from jax.sharding import PartitionSpec as P

RANK = 32
LANE = 128
F32 = jnp.float32
BF16 = jnp.bfloat16
MESH = pl.DeviceIdType.MESH
HIGHEST = lax.Precision.HIGHEST
NSUB = 4


def dot(a, b, precision=None):
    return lax.dot_general(
        a, b, (((1,), (0,)), ((), ())), precision=precision, preferred_element_type=F32
    )


def dot_t(a, b, precision=None):
    return lax.dot_general(
        a, b, (((1,), (1,)), ((), ())), precision=precision, preferred_element_type=F32
    )


def iota(shape, dim):
    return lax.broadcasted_iota(jnp.int32, shape, dim)


def split(x):
    high = x.astype(BF16)
    return high, (x - high.astype(F32)).astype(BF16)


def cosine(x):
    y = x * x
    p = jnp.full_like(y, -1.0 / 3628800.0)
    for coefficient in (1.0 / 40320.0, -1.0 / 720.0, 1.0 / 24.0, -0.5, 1.0):
        p = p * y + coefficient
    return p


def eliminate(a, steps):
    row = iota((RANK, LANE), 0)
    for k in steps:
        pivot_row = a[k : k + 1, :]
        column = a[:, k : k + 1]
        factor = column / a[k : k + 1, k : k + 1]
        a = a - jnp.where(row > k, factor * pivot_row, 0.0)
    return a


def inverse_factor(a):
    row, lane = iota((RANK, LANE), 0), iota((RANK, LANE), 1)
    diagonal = jnp.sum(jnp.where(row == lane, a, 0.0), axis=1, keepdims=True)
    scaled = a * lax.rsqrt(diagonal)
    return pltpu.roll(scaled, LANE - RANK, 1)[:, :RANK]


def kernel(
    shape,
    east_hbm,
    north_hbm,
    count_hbm,
    ids_ref,
    basis_ref,
    coeffs_ref,
    east_f,
    north_f,
    east_b,
    north_b,
    spread_signs,
    east_sketch,
    north_sketch,
    sketch,
    halo_send,
    halo_recv,
    edge_send,
    edge_recv,
    field,
    chain_send,
    chain_recv,
    whole,
    projection,
    gram_part,
    gram_slots,
    gram_x,
    gram_y,
    projection_x,
    projection_y,
    count_ref,
    load_sem,
    halo_ssem,
    halo_rsem,
    edge_ssem,
    edge_rsem,
    chain_ssem,
    chain_rsem,
    gather_ssem,
    gather_rsem,
    gram_ssem,
    gram_rsem,
    x_ssem,
    x_rsem,
    y_ssem,
    y_rsem,
):
    slots, rows, lons, n_tm, n_lat, n_x = shape
    n_y = n_lat // (2 * n_x)
    n_col = pl.cdiv(lons, LANE)
    tail = lons - (n_col - 1) * LANE
    padded = field.shape[1]
    width = n_col * LANE
    piece = width // NSUB
    total_rows = rows * n_lat
    cells = total_rows * lons

    m = lax.axis_index("tm")
    b = lax.axis_index("lat")
    core = lax.rem(b, 2)
    x = lax.rem(b // 2, n_x)
    y = b // (2 * n_x)
    south, north = {"lat": lax.rem(b + 1, n_lat)}, {"lat": lax.rem(b + n_lat - 1, n_lat)}

    def z_at(d):
        return {"tm": lax.rem(m + n_tm + d, n_tm)}

    def x_peer(i, sign=1):
        dx, flip = i // 2, i % 2
        other = core + flip - 2 * flip * core
        return lax.rem(x + n_x + sign * dx, n_x) * 2 + other

    def y_peer(d, sign=1):
        return lax.rem(y + n_y + sign * d, n_y)

    x_line = [{"lat": y * (2 * n_x) + x_peer(i)} for i in range(1, 2 * n_x)]
    y_line = [{"lat": y_peer(d) * (2 * n_x) + x * 2 + core} for d in range(1, n_y)]
    peers = [z_at(d) for d in (-2, -1, 1, 2)] + [south, north] + x_line + y_line
    barrier = pltpu.get_barrier_semaphore()
    for peer in peers:
        pl.semaphore_signal(barrier, inc=1, device_id=peer, device_id_type=MESH)

    def remote(src, dst, ssem, rsem, peer):
        return pltpu.make_async_remote_copy(
            src_ref=src, dst_ref=dst, send_sem=ssem, recv_sem=rsem, device_id=peer, device_id_type=MESH
        )

    middle = slots * rows // 2
    ends = [slice(0, middle), slice(middle, slots * rows)]
    loads = [pltpu.make_async_copy(count_hbm, count_ref, load_sem.at[3])]
    loads += [pltpu.make_async_copy(east_hbm.at[part], east_b.at[part], load_sem.at[i]) for i, part in enumerate(ends)]
    loads += [pltpu.make_async_copy(north_hbm, north_b, load_sem.at[2])]
    for copy in loads:
        copy.start()
    loads[0].wait()

    ids = jnp.broadcast_to(ids_ref[...], (RANK, slots))
    column = iota((RANK, slots), 0)
    mixed = ids * 1103515245 + column * 40503 + 12345
    mixed = jnp.bitwise_xor(mixed, jnp.right_shift(mixed, 13))
    mixed = mixed * 1664525 + 1013904223
    mixed = jnp.bitwise_xor(mixed, jnp.right_shift(mixed, 16))
    flipped = jnp.bitwise_and(jnp.right_shift(mixed, 7), 1)
    slot_used = iota((RANK, slots), 1) < count_ref[0]
    signs = jnp.where(slot_used, (1 - 2 * flipped).astype(F32), 0.0).astype(BF16)
    depth = slots * rows
    repeat = (iota((slots, depth), 1) // rows == iota((slots, depth), 0)).astype(F32).astype(BF16)
    repeated = dot(signs, repeat)
    lane_row = lax.rem(iota((RANK, depth), 1), rows)
    for j in range(rows):
        spread_signs[j * RANK : (j + 1) * RANK, :] = jnp.where(lane_row == j, repeated, 0.0).astype(BF16)

    band_row = iota((16, LANE), 0) + (b * rows - 1)
    cosines = cosine((total_rows // 2 - band_row).astype(F32) * (jnp.pi / 720.0))
    weights = 0.5 / jnp.sqrt(cosines)
    inside = jnp.logical_and(band_row >= 0, band_row < total_rows)
    cosines = jnp.where(inside, cosines, 0.0)

    for wide in (east_f, north_f):
        wide[:, depth:, :] = jnp.zeros((n_col, padded * rows - depth, LANE), F32)

    for i, part in enumerate(ends):
        loads[1 + i].wait()
        partial = dot(spread_signs[:, part], east_b[part, :]).reshape(rows, RANK, lons)
        if i > 0:
            partial = east_sketch[1 : rows + 1, :, 0:lons] + partial
        east_sketch[1 : rows + 1, :, 0:lons] = partial
    for side, j in ((0, 1), (1, rows)):
        halo_send[side] = east_sketch[j].astype(BF16)
    pl.semaphore_wait(barrier, len(peers))

    def cols(h):
        return pl.ds(h * piece, piece)

    halves = (list(range(0, NSUB // 2)), list(range(NSUB // 2, NSUB)))
    order = [h for pair in zip(halves[0], halves[1]) for h in pair]

    def halo(side, h):
        return remote(
            halo_send.at[side, :, cols(h)],
            halo_recv.at[1 - side, :, cols(h)],
            halo_ssem.at[side, h],
            halo_rsem.at[1 - side, h],
            (north, south)[side],
        )

    for h in order:
        for side in (0, 1):
            halo(side, h).start()
    loads[3].wait()
    north_sketch[:, :, 0:lons] = dot(spread_signs[...], north_b[...]).reshape(rows, RANK, lons)

    def roll_pair(tiles, lane):
        left = [pltpu.roll(t, LANE - 1, 1) for t in tiles]
        right = [pltpu.roll(t, 1, 1) for t in tiles]
        first_to_end = pltpu.roll(tiles[0], tail - 1, 1)
        end_to_first = pltpu.roll(tiles[-1], LANE - tail + 1, 1)
        result = []
        for c in range(n_col):
            if c < n_col - 1:
                nxt = jnp.where(lane < LANE - 1, left[c], left[c + 1])
            else:
                nxt = jnp.where(lane < tail - 1, left[c], first_to_end)
            prv = jnp.where(lane > 0, right[c], right[c - 1] if c > 0 else end_to_first)
            result.append(nxt - prv)
        return result

    def constants(j, count):
        def spread(t, i):
            return jnp.broadcast_to(t[i : i + 1, :], (count, LANE))

        return spread(cosines, j), spread(cosines, j + 2), spread(weights, j + 1)

    lane32 = iota((RANK, LANE), 1)

    def sketch_row(j):
        c_above, c_below, weight = constants(j, RANK)
        zonal = roll_pair([north_sketch[j, :, c * LANE : (c + 1) * LANE] for c in range(n_col)], lane32)
        for c in range(n_col):
            part = slice(c * LANE, (c + 1) * LANE)
            value = zonal[c]
            if j > 0:
                value = value - east_sketch[j, :, part] * c_above
            if j < rows - 1:
                value = value + east_sketch[j + 2, :, part] * c_below
            value = value * weight
            if c == n_col - 1:
                value = jnp.where(lane32 < tail, value, 0.0)
            sketch[j, :, part] = value

    def add_halo(side, h):
        halo(1 - side, h).wait_recv()
        j = (0, rows - 1)[side]
        c_above, c_below, weight = constants(j, RANK)
        scale = (-c_above * weight, c_below * weight)[side]
        for c in range(h * (piece // LANE), (h + 1) * (piece // LANE)):
            part = slice(c * LANE, (c + 1) * LANE)
            value = halo_recv[side, :, part].astype(F32) * scale
            if c == n_col - 1:
                value = jnp.where(lane32 < tail, value, 0.0)
            sketch[j, :, part] += value

    lane16 = iota((16, LANE), 1)

    def field_row(j, east_above, east_below):
        c_above, c_below, weight = constants(j, 16)

        def group(g, carry):
            part = pl.ds(g * (16 * rows) + j, 16, stride=rows)
            zonal = roll_pair([north_f[c, part, :] for c in range(n_col)], lane16)
            for c in range(n_col):
                value = (zonal[c] - east_above(g, c) * c_above + east_below(g, c) * c_below) * weight
                if c == n_col - 1:
                    value = jnp.where(lane16 < tail, value, 0.0)
                field[j, pl.ds(g * 16, 16), c * LANE : (c + 1) * LANE] = value.astype(BF16)
            return carry

        lax.fori_loop(0, padded // 16, group, 0)

    def local_east(j):
        return lambda g, c: east_f[c, pl.ds(g * (16 * rows) + j, 16, stride=rows), :]

    def halo_east(side):
        return lambda g, c: edge_recv[side, pl.ds(g * 16, 16), c * LANE : (c + 1) * LANE].astype(F32)

    def widen(flat, wide):
        def run():
            for c in range(n_col):
                w = LANE if c < n_col - 1 else tail
                wide[c, 0:depth, 0:w] = flat[:, c * LANE : c * LANE + w].astype(F32)

        return run

    def send_edges():
        for side, j in ((0, 0), (1, rows - 1)):
            for c in range(n_col):
                edge_send[side, :, c * LANE : (c + 1) * LANE] = east_f[
                    c, pl.ds(j, padded, stride=rows), :
                ].astype(BF16)
        for copy in edges:
            copy.start()

    edges = [
        remote(edge_send.at[0], edge_recv.at[1], edge_ssem.at[0], edge_rsem.at[1], north),
        remote(edge_send.at[1], edge_recv.at[0], edge_ssem.at[1], edge_rsem.at[0], south),
    ]

    def field_task(j):
        if 0 < j < rows - 1:
            return lambda: field_row(j, local_east(j - 1), local_east(j + 1))
        if j == 0:
            def run():
                edges[1].wait_recv()
                field_row(0, halo_east(0), local_east(1))
        else:
            def run():
                edges[0].wait_recv()
                field_row(j, local_east(j - 1), halo_east(1))
        return run

    tasks = [widen(east_b, east_f), send_edges, widen(north_b, north_f)]
    tasks += [field_task(j) for j in list(range(1, rows - 1)) + [0, rows - 1]]

    def work(count):
        for _ in range(min(count, len(tasks))):
            tasks.pop(0)()

    far, mid, near, summed = range(4)
    reach = (4, 3, 1, 2)
    route = (2, 1, 1, 2)
    toward = (-1, 1)
    pieces = ([h for pair in zip(halves[1], halves[0]) for h in pair], order)

    def row_at(offset):
        return lax.rem(m + n_tm + offset, n_tm)

    def chain(side, kind, h):
        return remote(
            chain_send.at[side, kind, :, cols(h)],
            chain_recv.at[side, kind, :, cols(h)],
            chain_ssem.at[side, kind, h],
            chain_rsem.at[side, kind, h],
            z_at(toward[side] * route[kind]),
        )

    def send_own(side, kind, h):
        j = row_at(toward[side] * reach[kind])
        chain_send[side, kind, :, cols(h)] = sketch[j, :, cols(h)].astype(BF16)
        chain(side, kind, h).start()

    def when_class(edge, offset, run):
        j = row_at(offset)
        is_edge = jnp.logical_or(j == 0, j == rows - 1)
        pl.when(is_edge if edge else jnp.logical_not(is_edge))(run)

    def begin(edge):
        for step in range(NSUB // 2):
            if edge:
                for h in order[2 * step : 2 * step + 2]:
                    for side in (0, 1):
                        add_halo(side, h)
            first = [pieces[side][2 * step] for side in (0, 1)]
            second = [pieces[side][2 * step + 1] for side in (0, 1)]
            for side in (0, 1):
                when_class(edge, toward[side] * reach[mid], lambda side=side: send_own(side, mid, first[side]))

            def send_far():
                for side in (0, 1):
                    send_own(side, far, second[side])

            when_class(edge, reach[far], send_far)
            for side in (0, 1):
                when_class(edge, toward[side] * reach[mid], lambda side=side: send_own(side, mid, second[side]))

    def begin_near(edge):
        for side in (0, 1):

            def run(side=side):
                for h in order:
                    send_own(side, near, h)

            when_class(edge, toward[side] * reach[near], run)

    def relay(edge):
        for i in range(NSUB):
            for side in (0, 1):

                def run(h=pieces[side][i], side=side):
                    j = row_at(toward[side] * 2)
                    value = sketch[j, :, cols(h)]
                    for kind in (mid, far) if h in halves[side] else (mid,):
                        chain(side, kind, h).wait_recv()
                        value = value + chain_recv[side, kind, :, cols(h)].astype(F32)
                    chain_send[side, summed, :, cols(h)] = value.astype(BF16)
                    chain(side, summed, h).start()

                when_class(edge, toward[side] * 2, run)

    to_one, to_two, to_three, to_four = range(4)
    stride_of = (1, 2, 1, 2)

    def gather(side, kind, h, j):
        return remote(
            whole.at[j, :, cols(h)],
            whole.at[j, :, cols(h)],
            gather_ssem.at[side, kind, h],
            gather_rsem.at[side, kind, h],
            z_at(toward[side] * stride_of[kind]),
        )

    def arrive(kind, edge):
        for h in order:
            for side in (0, 1):
                if kind == to_four and h not in halves[side]:
                    continue

                def run(h=h, side=side):
                    j = row_at(-toward[side] * (kind + 1))
                    gather(side, kind, h, j).wait_recv()
                    if kind == to_two:
                        if h in halves[side]:
                            gather(side, to_four, h, j).start()
                        gather(side, to_three, h, j).start()

                when_class(edge, -toward[side] * (kind + 1), run)

    def consume(j):
        projection[...] += dot_t(whole[j], field[j])

    class LatSum:
        def __init__(self, n, x_slots, y_slots):
            self.levels = (
                (x_slots, x_ssem.at[n], x_rsem.at[n], x * 2 + core, x_line, x_peer),
                (y_slots, y_ssem.at[n], y_rsem.at[n], y, y_line, y_peer),
            )

        def copy(self, level, i, slot):
            slots_of, ssem, rsem, _, line, _ = self.levels[level]
            return remote(slots_of.at[slot], slots_of.at[slot], ssem.at[i], rsem.at[i], line[i])

        def send(self, level, value):
            slots_of, _, _, here, line, _ = self.levels[level]
            slots_of[here] = value.astype(slots_of.dtype)
            for i in range(len(line)):
                self.copy(level, i, here).start()

        def total(self, level):
            slots_of, _, _, _, line, peer_of = self.levels[level]
            for i in range(len(line)):
                self.copy(level, i, peer_of(i + 1, -1)).wait_recv()
            value = slots_of[0].astype(F32)
            for i in range(1, len(line) + 1):
                value = value + slots_of[i].astype(F32)
            return value

        def drain(self):
            for level, (_, _, _, here, line, _) in enumerate(self.levels):
                for i in range(len(line)):
                    self.copy(level, i, here).wait_send()

    def gram_copy(d, slot):
        return remote(
            gram_slots.at[slot], gram_slots.at[slot], gram_ssem.at[d - 1], gram_rsem.at[d - 1],
            {"tm": lax.rem(m + d, n_tm)},
        )

    gram_sum, projection_sum = LatSum(0, gram_x, gram_y), LatSum(1, projection_x, projection_y)
    projection[...] = jnp.zeros(projection.shape, F32)

    for j in range(1, rows - 1):
        sketch_row(j)
    begin(False)
    for j in (0, rows - 1):
        sketch_row(j)
    work(3)
    begin(True)
    begin_near(False)
    work(1)
    relay(False)
    begin_near(True)
    work(1)
    relay(True)
    work(2)
    for h in order:
        value = sketch[m, :, cols(h)]
        for kind in (near, summed):
            for side in (0, 1):
                chain(side, kind, h).wait_recv()
                value = value + chain_recv[side, kind, :, cols(h)].astype(F32)
        whole[m, :, cols(h)] = value.astype(BF16)
        for side in (0, 1):
            gather(side, to_two, h, m).start()
    for h in order:
        for side in (0, 1):
            gather(side, to_one, h, m).start()
    own = whole[m]
    gram_part[...] = jnp.zeros((RANK, LANE), F32)
    gram_part[:, 0:RANK] = dot_t(own, own)
    gram_sum.send(0, gram_part[...])
    work(2)
    arrive(to_two, False)
    gram_sum.send(1, gram_sum.total(0))
    work(1)
    arrive(to_two, True)
    work(len(tasks))
    for offset in (0, -2, 2):
        consume(row_at(offset))
    gram_slots[m] = gram_sum.total(1)
    for d in range(1, n_tm):
        gram_copy(d, m).start()
    for kind, offset in ((to_one, 1), (to_three, 3)):
        for edge in (False, True):
            arrive(kind, edge)
        for side in (0, 1):
            consume(row_at(-toward[side] * offset))
    for edge in (False, True):
        arrive(to_four, edge)
    consume(row_at(4))
    projection_sum.send(0, projection[...])
    for d in range(1, n_tm):
        gram_copy(d, lax.rem(m + n_tm - d, n_tm)).wait_recv()
    gram = gram_slots[0]
    for i in range(1, n_tm):
        gram = gram + gram_slots[i]
    early = 14
    joined = jnp.where(iota((RANK, LANE), 1) == iota((RANK, LANE), 0) + RANK, 1.0, gram * (1.0 / cells))
    joined = eliminate(joined, range(early))
    projection_sum.send(1, projection_sum.total(0))
    inverse = inverse_factor(eliminate(joined, range(early, RANK - 1)))

    size = RANK * rows
    take_row = (iota((size, RANK), 0) // rows == iota((size, RANK), 1)).astype(F32).astype(BF16)
    take_col = (iota((RANK, size), 0) == lax.rem(iota((RANK, size), 1), RANK)).astype(F32).astype(BF16)
    same = lax.rem(iota((size, size), 0), rows) == iota((size, size), 1) // RANK
    flat = whole[...].reshape(size, width)
    basis = None
    for half in split(inverse):
        spread = dot(take_row, half).astype(BF16)
        spread = dot(spread, take_col)
        spread = jnp.where(same, spread, 0.0).astype(BF16)
        term = dot(spread, flat)
        basis = term if basis is None else basis + term
    basis_ref[...] = basis.reshape(RANK, rows, width)[:, :, :lons].astype(BF16)
    projected = projection_sum.total(1)
    coeffs = dot(inverse, projected, HIGHEST) * (1.0 / cells)
    coeffs = jnp.where(iota((RANK, padded), 1) < count_ref[0], coeffs, 0.0)
    coeffs_ref[...] = coeffs[:, :slots]

    for copy in edges:
        copy.wait_send()
    for side in (0, 1):
        for h in range(NSUB):
            halo(side, h).wait_send()
    for side in (0, 1):
        for kind in range(4):
            for h in range(NSUB):
                if kind != far or h in halves[side]:
                    chain(side, kind, h).wait_send()
                if kind != to_four or h in halves[side]:
                    gather(side, kind, h, m).wait_send()
    for part in (gram_sum, projection_sum):
        part.drain()
    for d in range(1, n_tm):
        gram_copy(d, m).wait_send()


def local(n_tm, n_lat, n_x, wind_east, wind_north, snap_counts, snap_ids):
    slots, rows, lons = wind_east.shape
    padded = -(-slots // LANE) * LANE
    n_col = -(-lons // LANE)
    width = n_col * LANE
    n_y = n_lat // (2 * n_x)
    ids = snap_ids.reshape(1, slots)
    shape = (slots, rows, lons, n_tm, n_lat, n_x)
    dma = pltpu.SemaphoreType.DMA
    return pl.pallas_call(
        functools.partial(kernel, shape),
        out_shape=(pltpu.VMEM((RANK, rows, lons), BF16), pltpu.VMEM((RANK, slots), F32)),
        in_specs=[
            pl.BlockSpec(memory_space=pl.ANY),
            pl.BlockSpec(memory_space=pl.ANY),
            pl.BlockSpec(memory_space=pltpu.HBM),
            pl.BlockSpec(memory_space=pltpu.VMEM),
        ],
        out_specs=(pl.BlockSpec(memory_space=pltpu.VMEM), pl.BlockSpec(memory_space=pltpu.VMEM)),
        scratch_shapes=[
            pltpu.VMEM((n_col, padded * rows, LANE), F32),
            pltpu.VMEM((n_col, padded * rows, LANE), F32),
            pltpu.VMEM((slots * rows, lons), BF16),
            pltpu.VMEM((slots * rows, lons), BF16),
            pltpu.VMEM((rows * RANK, slots * rows), BF16),
            pltpu.VMEM((rows + 2, RANK, width), F32),
            pltpu.VMEM((rows, RANK, width), F32),
            pltpu.VMEM((rows, RANK, width), F32),
            pltpu.VMEM((2, RANK, width), BF16),
            pltpu.VMEM((2, RANK, width), BF16),
            pltpu.VMEM((2, padded, width), BF16),
            pltpu.VMEM((2, padded, width), BF16),
            pltpu.VMEM((rows, padded, width), BF16),
            pltpu.VMEM((2, 4, RANK, width), BF16),
            pltpu.VMEM((2, 4, RANK, width), BF16),
            pltpu.VMEM((rows, RANK, width), BF16),
            pltpu.VMEM((RANK, padded), F32),
            pltpu.VMEM((RANK, LANE), F32),
            pltpu.VMEM((n_tm, RANK, LANE), F32),
            pltpu.VMEM((2 * n_x, RANK, LANE), F32),
            pltpu.VMEM((n_y, RANK, LANE), F32),
            pltpu.VMEM((2 * n_x, RANK, padded), BF16),
            pltpu.VMEM((n_y, RANK, padded), BF16),
            pltpu.SMEM((1,), jnp.int32),
            dma((4,)),
            dma((2, NSUB)),
            dma((2, NSUB)),
            dma((2,)),
            dma((2,)),
            dma((2, 4, NSUB)),
            dma((2, 4, NSUB)),
            dma((2, 4, NSUB)),
            dma((2, 4, NSUB)),
            dma((n_tm - 1,)),
            dma((n_tm - 1,)),
            dma((2, 2 * n_x - 1)),
            dma((2, 2 * n_x - 1)),
            dma((2, n_y - 1)),
            dma((2, n_y - 1)),
        ],
        compiler_params=pltpu.CompilerParams(
            collective_id=0, has_side_effects=True, vmem_limit_bytes=60 * 1024 * 1024
        ),
        name="eof",
    )(
        wind_east.reshape(slots * rows, lons), wind_north.reshape(slots * rows, lons), snap_counts, ids
    )


def solution(mesh):
    in_specs = (P("tm", "lat", None), P("tm", "lat", None), P("tm"), P("tm"))
    out_specs = (P(None, "lat", None), P(None, "tm"))
    body = functools.partial(local, mesh.shape["tm"], mesh.shape["lat"], 4)
    return jax.shard_map(body, mesh=mesh, in_specs=in_specs, out_specs=out_specs, check_vma=False)
```
